32 devices in a mesh: groups: 2 (over y), ctx: 4 (over z), tp: 2 (over x), dp: 2 (over core).
Axes of the slice: x: 2, y: 2, z: 4, core: 2. Of those that a mesh axis runs over, the one named last changes fastest.
Arguments:
- x_in: bfloat16 [4096, 8192], P(('groups', 'ctx', 'dp'), 'tp'), parts along dimension 0, may hold values from -6 to 6
- bc_in: bfloat16 [4096, 2, 1024], P(('groups', 'ctx', 'dp'), None, 'tp'), parts along dimension 0, may hold values from -6 to 6
- gate_z: bfloat16 [4096, 8192], P(('groups', 'ctx', 'dp'), 'tp'), parts along dimension 0, may hold values from -60 to 60
- log_decay: float32 [2, 4096, 128], P(None, ('groups', 'ctx', 'dp'), 'tp'), parts along dimension 1, may hold values from -1 to 0
- resets: int32 [4096], P(('groups', 'ctx', 'dp')), parts along dimension 0, may hold values from 0 to 1, as said below
- conv_x: float32 [4, 8192], P(None, 'tp'), may hold values from -3 to 3
- conv_bc: float32 [4, 2, 1024], P(None, None, 'tp'), may hold values from -1.8 to 1.8
- skip_d: float32 [128], P('tp'), may hold values from 0.25 to 2
- norm_gain: float32 [8192], P('tp'), may hold values from 0.5 to 1.5
- visit_span: int32 [256, 2], P(('groups', 'ctx', 'dp')), parts along dimension 0, may hold values from 0 to 2048, as said below
Outputs:
- token_out: bfloat16 [4096, 8192], P(('groups', 'ctx', 'dp'), 'tp'), parts along dimension 0
- pooled: bfloat16 [256, 8192], P(('groups', 'ctx', 'dp'), 'tp'), parts along dimension 0
The draws below stay inside these ranges and needn't reach their ends.
There are 2 independent parts, one for each index of `groups`. The reference program is written for one: setup_inputs(seed, part) draws one part's arguments, and reference() takes and returns one part's arrays. A program takes and returns all parts, laid end to end along the dimension named above; an argument that names none is the same for every part. Nothing has to cross between parts.
Inputs may be any that keep to these rules, and one draw needn't show every extreme that they name: `resets`: at most 3 tokens carry a 1, never token 0; a 1 opens a new patient stream. `visit_span`: the visits in rows k * 16 to (k + 1) * 16 - 1 begin in tokens k * 256 to (k + 1) * 256 - 1; every visit holds 1 to 256 tokens and some visit holds exactly 256; visits may intersect.
All inputs are finite; a program needn't handle non-finite values.
Results may differ from the reference program's by a relative error of at most 0.0036.
Values may be sent and summed in bfloat16 or wider, within the bound.
A program may use at most 128 MiB of HBM per device.

```python
import math
import jax
import jax.numpy as jnp
from jax import lax

HEADS = 128
HEADDIM = 64
STATE = 128
GROUPS = 8
CONV = 4
INNER = 8192
TOK_DEV = 256
STRETCH = 256
VISLEN = 256
VIS_DEV = 16
WINDOW_TOKENS = 2048
VISITS = 128


def draw_log_decay(key, part):
    key_sequence = jax.random.split(key, 7)
    fast_share = 0.5
    fast_heads = jax.random.uniform(key_sequence[0], (2, HEADS)) < fast_share
    fast_rate = jnp.exp(jax.random.uniform(key_sequence[1], (2, HEADS), minval=math.log(1.0 / 50.0), maxval=math.log(1.0 / 30.0)))
    slow_rate = jnp.exp(jax.random.uniform(key_sequence[2], (2, HEADS), minval=math.log(0.1), maxval=0.0)) / WINDOW_TOKENS
    head_decay_rate = jnp.where(fast_heads, fast_rate, slow_rate)
    block_count = WINDOW_TOKENS // TOK_DEV
    block_multiplier = jnp.exp(jax.random.uniform(key_sequence[3], (2, block_count, HEADS), minval=math.log(0.5), maxval=math.log(2.0)))
    block_multiplier = jnp.repeat(block_multiplier, TOK_DEV, axis=1)
    token_multiplier = jnp.exp(jax.random.uniform(key_sequence[4], (2, WINDOW_TOKENS, HEADS), minval=math.log(0.5), maxval=math.log(2.0)))
    spike_location = jax.random.randint(key_sequence[5], (2, 2), 0, WINDOW_TOKENS)
    spike_magnitude = jax.random.uniform(key_sequence[6], (2, 2), minval=0.22, maxval=0.69)
    token_position = jnp.arange(WINDOW_TOKENS)
    spike_penalty = jnp.sum((token_position[None, None, :] == spike_location[:, :, None]).astype(jnp.float32) * spike_magnitude[:, :, None], axis=1)
    return -(head_decay_rate[:, None, :] * block_multiplier * token_multiplier) - spike_penalty[:, :, None]


def draw_resets(key, part):
    where_at = jax.random.randint(key, (3,), 1, WINDOW_TOKENS)
    token_position = jnp.arange(WINDOW_TOKENS)
    return jnp.any(token_position[:, None] == where_at[None, :], axis=1).astype(jnp.int32)


def draw_gate_z(key, part):
    key_sequence = jax.random.split(key, 3)
    row_scale = jnp.exp(jax.random.uniform(key_sequence[0], (WINDOW_TOKENS, 1), minval=math.log(0.3), maxval=math.log(3.0)))
    col_scale = jnp.exp(jax.random.uniform(key_sequence[1], (1, INNER), minval=math.log(0.3), maxval=math.log(3.0)))
    base = jnp.clip(jax.random.normal(key_sequence[2], (WINDOW_TOKENS, INNER)), -6.0, 6.0)
    return (base * row_scale * col_scale).astype(jnp.bfloat16)


def draw_visit_span(key, part):
    key_sequence = jax.random.split(key, 3)
    index = jnp.arange(VISITS)
    owner_block = index // VIS_DEV
    span_len = jax.random.randint(key_sequence[0], (VISITS,), 1, VISLEN + 1)
    longest = jax.random.randint(key_sequence[1], (), 0, VISITS)
    span_len = jnp.where(index == longest, VISLEN, span_len)
    block_last = index % VIS_DEV == VIS_DEV - 1
    span_len = jnp.where(block_last, VISLEN, span_len)
    offset_in = jax.random.randint(key_sequence[2], (VISITS,), 0, TOK_DEV)
    offset_in = jnp.where(block_last, TOK_DEV - 1, offset_in)
    begin = jnp.minimum(owner_block * TOK_DEV + offset_in, WINDOW_TOKENS - span_len)
    begin = jnp.where(index == 0, 0, begin)
    begin = jnp.where(index == VISITS - 1, WINDOW_TOKENS - span_len, begin)
    return jnp.stack([begin, begin + span_len], axis=1).astype(jnp.int32)


def levels(key, dims, cuts, least, top_value):
    factor_of = 1.0
    for axis_at, parts in cuts:
        steps = jax.random.uniform(jax.random.fold_in(jax.random.fold_in(key, 6), axis_at), (parts,), jnp.float32, least / len(cuts), top_value / len(cuts))
        factor_of = factor_of * jnp.repeat(jnp.exp(steps), dims[axis_at] // parts).reshape((-1,) + (1,) * (len(dims) - 1 - axis_at))
    return factor_of


def gaussian(key, dims, scale, most, cuts=(), kind=jnp.bfloat16):
    result = jax.random.normal(key, dims, jnp.float32) * scale
    if len(cuts) > 0:
        result = levels(key, dims, cuts, -0.22, 0.18) * result
    return jnp.clip(result, min=-most, max=most).astype(kind)


def setup_inputs(seed: int = 0, part: int = 0) -> dict:
    seeds = jax.random.split(jax.random.key(seed), 11)
    own_keys = jax.random.split(jax.random.fold_in(seeds[10], part), 11)
    return {
        "x_in": gaussian(own_keys[0], (WINDOW_TOKENS, INNER), 1.0, 6.0, ((0, 8), (1, 2))),
        "bc_in": gaussian(own_keys[1], (WINDOW_TOKENS, 2, GROUPS * STATE), 1.0, 6.0, ((0, 8), (2, 2))),
        "gate_z": draw_gate_z(jax.random.fold_in(jax.random.fold_in(seeds[10], part), 71), part),
        "log_decay": draw_log_decay(jax.random.fold_in(jax.random.fold_in(seeds[10], part), 71), part),
        "resets": draw_resets(jax.random.fold_in(jax.random.fold_in(seeds[10], part), 71), part),
        "conv_x": gaussian(seeds[5], (CONV, INNER), 0.5, 3.0, ((1, 2),), jnp.float32),
        "conv_bc": gaussian(seeds[6], (CONV, 2, GROUPS * STATE), 0.3, 1.8, ((2, 2),), jnp.float32),
        "skip_d": jnp.clip(0.25 + 1.75 * jax.random.uniform(seeds[7], (HEADS,), jnp.float32) ** levels(seeds[7], (HEADS,), ((0, 2),), -0.2, 0.2), 0.25, 2.0),
        "norm_gain": jnp.clip(1.0 + 0.1 * jax.random.normal(seeds[8], (INNER,), jnp.float32), 0.5, 1.5),
        "visit_span": draw_visit_span(jax.random.fold_in(jax.random.fold_in(seeds[10], part), 71), part),
    }


def conv_silu(signal, rim, weight):
    kernel = weight.shape[0]
    length = signal.shape[0]
    padded = jnp.concatenate([rim, signal], axis=0).astype(jnp.float32)
    summed = weight[0] * padded[0:length]
    for offset in range(1, kernel):
        summed = summed + weight[offset] * padded[offset:offset + length]
    return jax.nn.silu(summed).astype(jnp.bfloat16)

def input_weight(log_rate):
    return jnp.sqrt(-jnp.expm1(2.0 * log_rate))

def stretch_parts(x_block, b_block, c_block, log_block, break_block, scale_block, strict):
    length = x_block.shape[0]
    per_group = x_block.shape[1] // b_block.shape[1]
    cumul = jnp.cumsum(log_block, axis=0)
    segment = jnp.cumsum(break_block)
    token_position = jnp.arange(length)
    if strict:
        ordered = token_position[:, None] > token_position[None, :]
    else:
        ordered = token_position[:, None] >= token_position[None, :]
    keeping = (ordered & (segment[:, None] == segment[None, :]))[None]
    cumul_t = cumul.T
    spread = jnp.where(keeping, cumul_t[:, :, None] - cumul_t[:, None, :], 0.0)
    decays = jnp.where(keeping, jnp.exp(spread), 0.0)
    scores = jnp.einsum('ign,jgn->gij', c_block.astype(jnp.float32), b_block.astype(jnp.float32))
    scores = jnp.repeat(scores, per_group, axis=0)
    mixing = (scores * decays * scale_block.T[:, None, :]).astype(jnp.bfloat16)
    y_inner = jnp.einsum('hij,jhp->ihp', mixing.astype(jnp.float32), x_block.astype(jnp.float32))
    same_end = (segment[-1] == segment).astype(jnp.float32)
    to_end = jnp.exp(cumul[-1][None, :] - cumul) * same_end[:, None] * scale_block
    weighted = (x_block.astype(jnp.float32) * to_end[:, :, None]).astype(jnp.bfloat16)
    b_heads = jnp.repeat(b_block, per_group, axis=1)
    stretch_state = jnp.einsum('jhp,jhn->hpn', weighted.astype(jnp.float32), b_heads.astype(jnp.float32))
    carried = jnp.exp(cumul[-1]) * (segment[-1] == 0).astype(jnp.float32)
    leading = jnp.exp(cumul) * (segment == 0).astype(jnp.float32)[:, None]
    return (y_inner, stretch_state, carried, leading)

def direction_sweep(x_heads, b_mat, c_mat, log_rate, break_flags, scales, strict):
    stretches = x_heads.shape[0] // STRETCH
    per_group = x_heads.shape[1] // b_mat.shape[1]

    def blocks(array):
        return array.reshape((stretches, STRETCH) + array.shape[1:])

    def advance(state_now, pieces):
        y_inner, stretch_state, carried, leading = stretch_parts(*pieces, strict)
        c_heads = jnp.repeat(pieces[2], per_group, axis=1).astype(jnp.float32)
        from_state = jnp.einsum('ihn,hpn->ihp', c_heads, state_now, precision=lax.Precision.HIGHEST)
        return (carried[:, None, None] * state_now + stretch_state, y_inner + leading[:, :, None] * from_state)
    initial = jnp.zeros((x_heads.shape[1], x_heads.shape[2], b_mat.shape[2]), jnp.float32)
    pieces = tuple((blocks(a) for a in (x_heads, b_mat, c_mat, log_rate, break_flags, scales)))
    _, outputs = lax.scan(advance, initial, pieces)
    return outputs.reshape(x_heads.shape)

def reference(x_in, bc_in, gate_z, log_decay, resets, conv_x, conv_bc, skip_d, norm_gain, visit_span):
    kernel = conv_x.shape[0]
    x_conv = conv_silu(x_in, jnp.zeros((kernel - 1, x_in.shape[1]), jnp.bfloat16), conv_x)
    bc_conv = conv_silu(bc_in, jnp.zeros((kernel - 1,) + bc_in.shape[1:], jnp.bfloat16), conv_bc)
    x_heads = x_conv.reshape(WINDOW_TOKENS, HEADS, HEADDIM)
    b_mat = bc_conv[:, 0].reshape(WINDOW_TOKENS, GROUPS, STATE)
    c_mat = bc_conv[:, 1].reshape(WINDOW_TOKENS, GROUPS, STATE)
    forward_log = log_decay[0]
    backward_log = log_decay[1]
    y_fwd = direction_sweep(x_heads, b_mat, c_mat, forward_log, resets, input_weight(forward_log), False)
    rev_log = jnp.concatenate([jnp.zeros((1, HEADS), jnp.float32), jnp.flip(backward_log, 0)[:-1]], axis=0)
    rev_break = jnp.concatenate([jnp.zeros((1,), jnp.int32), jnp.flip(resets, 0)[:-1]], axis=0)
    y_rev = direction_sweep(jnp.flip(x_heads, 0), jnp.flip(b_mat, 0), jnp.flip(c_mat, 0), rev_log, rev_break, jnp.flip(input_weight(backward_log), 0), True)
    mixed = y_fwd + jnp.flip(y_rev, 0) + skip_d[None, :, None] * x_heads.astype(jnp.float32)
    group_width = INNER // GROUPS
    gated = mixed.reshape(WINDOW_TOKENS, GROUPS, group_width) * jax.nn.silu(gate_z.astype(jnp.float32)).reshape(WINDOW_TOKENS, GROUPS, group_width)
    mean_sq = lax.optimization_barrier(jnp.mean(gated * gated, axis=2, keepdims=True))
    normed = (gated * lax.rsqrt(mean_sq + 1e-05)).reshape(WINDOW_TOKENS, INNER) * norm_gain
    token_out = normed.astype(jnp.bfloat16)
    token_position = jnp.arange(WINDOW_TOKENS)
    inside = ((token_position[None, :] >= visit_span[:, 0:1]) & (token_position[None, :] < visit_span[:, 1:2])).astype(jnp.bfloat16)
    sums = jnp.dot(inside, token_out, preferred_element_type=jnp.float32)
    pooled = (sums / (visit_span[:, 1:2] - visit_span[:, 0:1]).astype(jnp.float32)).astype(jnp.bfloat16)
    return (token_out, pooled)
```

```python
import functools
import jax
import jax.numpy as jnp
from jax import lax
from jax.experimental import pallas as pl
from jax.experimental.pallas import tpu as pltpu
from jax.sharding import PartitionSpec as P

HEADDIM = 64
STATE = 128
GROUPS = 8
PER = 16
PARTS = 4
LOG2E = 1.4426950408889634
BIG = 160.0
LIMIT = 60
HALO = 8
LAG = 2
MESH = pl.DeviceIdType.MESH


def silu(v):
    half = 0.5 * v
    return half + half * jnp.tanh(half)


def conv(padded, taps):
    total = taps[3] * padded[HALO:]
    for k in range(3):
        total = total + taps[k] * pltpu.roll(padded, 3 - k, 0)[HALO:]
    return silu(total)


def dot(a, b):
    return jnp.dot(a, b, preferred_element_type=jnp.float32)


def kernel(
    chips,
    groups,
    x_hbm, bc_hbm, gate_hbm, rate_hbm, reset_hbm, taps_x_hbm, taps_bc_hbm, skip_hbm, gain_hbm, span_hbm,
    out_ref, pool_ref,
    x_ref, bc_ref, gate_ref, rate_ref, reset_ref, taps_x, taps_bc, skip_ref, gain_ref, span_ref,
    halo_x, span_in, bc_wide, xc, bs, bt, cs, colt, rowt, weights, ends, expand, spreads, sent, skips, y_acc, squares, h_lead,
    s_made, s_in, chain_in, follow_in, chain_out,
    own_pool, spill_out, spill_in,
    sem_in, sem_x, sem_halo, sem_s, sem_chain, sem_follow, sem_spill,
):
    tokens = x_ref.shape[0]
    width = PER * HEADDIM
    half = tokens // 2
    part = width // PARTS
    chunks = PARTS * groups
    pairs = 2 * groups
    c = lax.axis_index("ctx")
    d = lax.axis_index("dp")
    other = 1 - d
    nxt = c + 2 * d - 1
    prv = c - 2 * d + 1
    pos = d * c + (1 - d) * (chips - 1 - c)
    has_next = pos < chips - 1
    has_prev = pos > 0
    index = c * 2 + d
    last_index = chips * 2 - 1
    partner = {"ctx": c, "dp": other}
    halo_to = {"ctx": d * nxt + (1 - d) * c, "dp": other}
    spill_to = {"ctx": d * c + (1 - d) * nxt, "dp": other}
    follow_chain = {"ctx": nxt, "dp": d}

    bc_main = bc_ref.at[pl.ds(HALO * pairs, tokens * pairs)]
    sources = (rate_hbm, reset_hbm, bc_hbm, taps_bc_hbm, taps_x_hbm, gate_hbm, skip_hbm, gain_hbm, span_hbm)
    places = (rate_ref, reset_ref, bc_main, taps_bc, taps_x, gate_ref, skip_ref, gain_ref, span_ref)
    loads = [pltpu.make_async_copy(sources[k], places[k], sem_in.at[k]) for k in range(9)]

    def x_load(g):
        wide = pl.ds(pl.multiple_of(g * width, width), width)
        return pltpu.make_async_copy(x_hbm.at[:, wide], x_ref.at[:, wide], sem_x.at[g])

    for load in loads[:5]:
        load.start()
    x_load(0).start()

    barrier = pltpu.get_barrier_semaphore()
    pl.semaphore_signal(barrier, inc=1, device_id=partner, device_id_type=MESH)

    @pl.when(has_next)
    def _():
        pl.semaphore_signal(barrier, inc=1, device_id={"ctx": nxt, "dp": other}, device_id_type=MESH)
        pl.semaphore_signal(barrier, inc=1, device_id={"ctx": nxt, "dp": d}, device_id_type=MESH)

    @pl.when(has_prev)
    def _():
        pl.semaphore_signal(barrier, inc=1, device_id={"ctx": prv, "dp": d}, device_id_type=MESH)

    rows = lax.broadcasted_iota(jnp.int32, (tokens, tokens), 0)
    cols = lax.broadcasted_iota(jnp.int32, (tokens, tokens), 1)
    upto = (rows <= cols).astype(jnp.float32).astype(jnp.bfloat16)
    erow = lax.broadcasted_iota(jnp.int32, (8 * PER, width), 0)
    ehead = lax.div(lax.broadcasted_iota(jnp.int32, (8 * PER, width), 1), HEADDIM)
    for which in range(4):
        least = 4 * PER * (which // 2)
        near = lax.rem(erow, 2 * PER) == ehead + PER * (1 - which % 2)
        near = near & (erow >= least) & (erow < least + 4 * PER)
        at = (which % 2) * width
        expand[which // 2, :, at : at + width] = near.astype(jnp.float32).astype(jnp.bfloat16)

    @pl.when(pos == 0)
    def _():
        chain_in[...] = jnp.zeros_like(chain_in)

    @pl.when(pos == chips - 1)
    def _():
        follow_in[...] = jnp.zeros_like(follow_in)

    @pl.when(index == 0)
    def _():
        halo_x[...] = jnp.zeros_like(halo_x)
        bc_ref[: HALO * pairs] = jnp.zeros((HALO * pairs, STATE), jnp.bfloat16)
        span_in[...] = jnp.zeros_like(span_in)

    pl.semaphore_wait(barrier, 1 + 2 * has_next.astype(jnp.int32) + has_prev.astype(jnp.int32))

    def remote(src, dst, sems, k, to):
        return pltpu.make_async_remote_copy(
            src_ref=src, dst_ref=dst, send_sem=sems.at[0, k], recv_sem=sems.at[1, k],
            device_id=to, device_id_type=MESH,
        )

    halos = (
        remote(bc_hbm.at[pl.ds((tokens - HALO) * pairs, HALO * pairs)], bc_ref.at[pl.ds(0, HALO * pairs)],
               sem_halo, 0, halo_to),
        remote(x_hbm.at[pl.ds(tokens - HALO, HALO)], halo_x, sem_halo, 1, halo_to),
        remote(span_hbm, span_in, sem_halo, 2, halo_to),
    )

    @pl.when(index < last_index)
    def _():
        for copy in halos:
            copy.start()

    for g in range(1, groups):
        x_load(g).start()

    def s_copy(q):
        return remote(s_made.at[0, q], s_in.at[q], sem_s, q, partner)

    def chain_copy(q):
        return remote(chain_out.at[q], chain_in.at[q], sem_chain, q, follow_chain)

    def follow_copy(q):
        return remote(chain_in.at[q], follow_in.at[q], sem_follow, q, partner)

    def spill_copy(g):
        return remote(spill_out.at[g], spill_in.at[g], sem_spill, g, spill_to)

    for load in loads[:2]:
        load.wait()

    def hi_lo(v):
        hi = v.astype(jnp.bfloat16).astype(jnp.float32)
        return jnp.concatenate([hi, v - hi], axis=0)

    fold = BIG * reset_ref[...].astype(jnp.float32)
    heads = groups * PER
    rate = jnp.concatenate([rate_ref[0], rate_ref[1]], axis=0)
    step = rate * LOG2E - fold
    step_hi = step.astype(jnp.bfloat16)
    rest = step - step_hi.astype(jnp.float32)
    step_mid = rest.astype(jnp.bfloat16)
    step_lo = (rest - step_mid.astype(jnp.float32)).astype(jnp.bfloat16)
    sums = dot(jnp.concatenate([step_hi, step_mid, step_lo], axis=0), upto)
    cum = sums[: 2 * heads] + (sums[2 * heads : 4 * heads] + sums[4 * heads :])
    is_fwd = lax.broadcasted_iota(jnp.int32, (2 * heads, tokens), 0) < heads
    r = -2.0 * rate
    small = r * (1.0 - r * (1 / 2 - r * (1 / 6 - r * (1 / 24 - r * (1 / 120 - r / 720)))))
    loss = jnp.where(r < 0.25, small, 1.0 - jnp.exp(-r))
    log_weight = jnp.maximum((0.5 * LOG2E) * jnp.log(loss), -1000.0)
    col = jnp.where(is_fwd, cum, -cum)
    row = log_weight - col
    end = cum[:, tokens - 1 : tokens]
    to_end = jnp.exp2(row + jnp.where(is_fwd, end, 0.0))
    lead = jnp.exp2(jnp.where(is_fwd, cum, end - cum))
    total = jnp.broadcast_to(jnp.exp2(end), (2 * heads, 128))

    def of_group(v, g):
        return jnp.concatenate([v[g * PER : (g + 1) * PER], v[heads + g * PER : heads + (g + 1) * PER]], axis=0)

    for g in range(groups):
        colt[g] = of_group(col, g).T
        rowt[g] = of_group(row, g)
        ends[g] = of_group(total, g)
        both = jnp.concatenate([hi_lo(of_group(to_end, g)), hi_lo(of_group(lead, g))], axis=0)
        weights[g] = both.T.astype(jnp.bfloat16)

    for load in loads[2:5]:
        load.wait()

    def lanes(k):
        return slice(k * part, (k + 1) * part)

    def lanes_of(which, k):
        return slice(which * width + k * part, which * width + (k + 1) * part)

    def spread_end(g, which, k):
        picked = expand[0, : 2 * PER, lanes_of(which, k)].astype(jnp.float32) * ends[g, :, :1]
        return jnp.broadcast_to(jnp.sum(picked, axis=0, keepdims=True), (8, part))

    def end_of(block):
        return block[STATE : STATE + 1].astype(jnp.float32) + block[STATE + 8 : STATE + 9].astype(jnp.float32)

    def relay(q):
        s_copy(q).wait_recv()

        @pl.when(has_prev)
        def _():
            chain_copy(q).wait_recv()
            follow_copy(q).start()

        near = s_in[q]
        state = end_of(near) * chain_in[q].astype(jnp.float32) + near[:STATE].astype(jnp.float32)
        h_lead[q] = state.astype(jnp.bfloat16)

        @pl.when(has_next)
        def _():
            own = s_made[1, q]
            chain_out[q] = (end_of(own) * state + own[:STATE].astype(jnp.float32)).astype(jnp.bfloat16)
            chain_copy(q).start()

    span = 32
    per_tap = [jnp.concatenate([taps_bc[k * pairs : (k + 1) * pairs]] * (span), axis=0) for k in range(4)]

    def conv_bc(t):
        at = pl.multiple_of(t * span * pairs, span * pairs)
        raw = bc_ref[pl.ds(at, (span + HALO) * pairs)].astype(jnp.float32)
        total = per_tap[3] * raw[HALO * pairs :]
        for k in range(3):
            back = (HALO - 3 + k) * pairs
            total = total + per_tap[k] * raw[back : back + span * pairs]
        bc_wide[pl.ds(at, span * pairs)] = silu(total)

    @pl.loop(1, tokens // span)
    def _(t):
        conv_bc(t)

    @pl.when(index > 0)
    def _():
        for copy in halos:
            copy.wait_recv()

    conv_bc(0)
    for load in loads[5:]:
        load.start()

    for g in range(groups):
        b_g = bc_wide[pl.ds(2 * g, tokens, stride=pairs), :]
        bs[g] = b_g.astype(jnp.bfloat16)
        bt[g] = b_g.T.astype(jnp.bfloat16)
        cs[g] = bc_wide[pl.ds(2 * g + 1, tokens, stride=pairs), :].astype(jnp.bfloat16)

    @pl.loop(0, groups)
    def _(g):
        x_load(g).wait()
        spreads[...] = dot(weights[g], expand[0])
        for k in range(PARTS):
            wide = pl.ds(pl.multiple_of(g * width + k * part, part), part)
            padded = jnp.concatenate([halo_x[:, wide].astype(jnp.float32), x_ref[:, wide].astype(jnp.float32)], axis=0)
            x_g = conv(padded, [taps_x[j : j + 1, wide] for j in range(4)]).astype(jnp.bfloat16)
            xc[g, :, lanes(k)] = x_g
            xf = x_g.astype(jnp.float32)
            for which in range(2):
                sent[:, lanes_of(which, k)] = (xf * spreads[:, lanes_of(which, k)]).astype(jnp.bfloat16)
        made = dot(bt[g], sent[...]).astype(jnp.bfloat16)
        for k in range(PARTS):
            q = g * PARTS + k
            for which in range(2):
                role = d if which == 0 else other
                s_made[1 - role, q, :STATE] = made[:, lanes_of(which, k)]
                s_made[1 - role, q, STATE:] = hi_lo(spread_end(g, which, k)).astype(jnp.bfloat16)
            s_copy(q).start()

        @pl.when(pos == 0)
        def _():
            @pl.loop(jnp.maximum(g * PARTS - LAG, 0), (g + 1) * PARTS - LAG)
            def _(q):
                relay(q)

    @pl.when(pos == 0)
    def _():
        @pl.loop(max(chunks - LAG, 0), chunks)
        def _(q):
            relay(q)

    early = jnp.where(d == 0, 1170 + 380 * (pos - 1), 950 + 220 * (pos - 1))

    def due(unit):
        by = jnp.clip(lax.div(1150 + 47 * unit - early + 7800, 78) - 99, 0, chunks)
        return jnp.where(pos == 0, chunks, by)

    left = lax.broadcasted_iota(jnp.int32, (tokens, 128), 1) < HEADDIM
    lower = rows[:half, :half] >= cols[:half, :half]

    @pl.loop(0, groups)
    def _(g):
        score = lax.dot_general(cs[g], bs[g], (((1,), (1,)), ((), ())), preferred_element_type=jnp.float32)
        for quarter in range(4):
            unit = 4 * g + quarter
            @pl.loop(jnp.where(unit == 0, jnp.where(pos == 0, chunks, 0), due(unit - 1)), due(unit))
            def _(q):
                relay(q)

            for pair in range(quarter * PER // 8, (quarter + 1) * PER // 8):
                at = pair * 2 * HEADDIM
                x_pair = xc[g, :, at : at + 2 * HEADDIM]
                got = []
                for head in (2 * pair, 2 * pair + 1):
                    cf = colt[g, :, head : head + 1]
                    cb = colt[g, :, PER + head : PER + head + 1]
                    rf = rowt[g, head : head + 1, :]
                    rb = rowt[g, PER + head : PER + head + 1, :]
                    tl = jnp.where(lower, cf[:half] + rf[:, :half], cb[:half] + rb[:, :half])
                    tr = cb[:half] + rb[:, half:]
                    bl = cf[half:] + rf[:, :half]
                    br = jnp.where(lower, cf[half:] + rf[:, half:], cb[half:] + rb[:, half:])
                    top = jnp.concatenate([tl, tr], axis=1)
                    bottom = jnp.concatenate([bl, br], axis=1)
                    mix_top = (score[:half] * jnp.exp2(top)).astype(jnp.bfloat16)
                    mix_bottom = (score[half:] * jnp.exp2(bottom)).astype(jnp.bfloat16)
                    got.append(dot(jnp.concatenate([mix_top, mix_bottom], axis=0), x_pair))
                y_acc[g, :, at : at + 2 * HEADDIM] = jnp.where(left, got[0], got[1])

    for load in loads[5:]:
        load.wait()

    vis = span_ref.shape[1]
    token = index * tokens + lax.broadcasted_iota(jnp.int32, (tokens, vis), 0)

    def covers(ref):
        return ((token >= ref[0:1]) & (token < ref[1:2])).astype(jnp.float32).T

    inside = jnp.concatenate([covers(span_ref), covers(span_in)], axis=0).astype(jnp.bfloat16)
    same = lax.broadcasted_iota(jnp.int32, (vis, vis), 0) == lax.broadcasted_iota(jnp.int32, (vis, vis), 1)
    spanned = jnp.maximum(span_ref[1:2] - span_ref[0:1], 1).astype(jnp.float32)
    length = jnp.sum(jnp.where(same, spanned, 0.0), axis=1, keepdims=True)

    @pl.loop(0, groups)
    def _(g):
        at = lax.broadcasted_iota(jnp.int32, (groups * PER, width), 0)
        head = lax.div(lax.broadcasted_iota(jnp.int32, (groups * PER, width), 1), HEADDIM)
        pick = (at == head + g * PER).astype(jnp.float32)
        skips[g] = lax.dot(jnp.broadcast_to(skip_ref[...], (8, groups * PER)), pick,
                           precision=lax.Precision.HIGHEST, preferred_element_type=jnp.float32)

    before = due(4 * groups - 1)

    def reached(step):
        further = before + lax.div(3 * step, 4) + 1
        return jnp.clip(jnp.maximum(step + 1, jnp.where(has_next, further, before)), 0, chunks)

    @pl.loop(0, groups)
    def _(g):
        spreads[...] = dot(weights[g], expand[1])
        for k in range(PARTS):
            q = g * PARTS + k

            @pl.loop(jnp.where(q == 0, before, reached(q - 1)), reached(q))
            def _(p):
                relay(p)

            @pl.when(has_next)
            def _():
                follow_copy(q).wait_recv()

            wide = pl.ds(pl.multiple_of(g * width + k * part, part), part)
            c_g = cs[g]
            near = pl.ds(pl.multiple_of(d * width + k * part, part), part)
            far = pl.ds(pl.multiple_of(other * width + k * part, part), part)
            lead = spreads[:, near] * dot(c_g, h_lead[q]) + spreads[:, far] * dot(c_g, follow_in[q])
            mixed = y_acc[g, :, lanes(k)] + lead + skips[g, 0:1, lanes(k)] * xc[g, :, lanes(k)].astype(jnp.float32)
            gated = mixed * silu(gate_ref[:, wide].astype(jnp.float32))
            y_acc[g, :, lanes(k)] = gated
            square = gated * gated
            folded = square[:, :128]
            for n in range(1, part // 128):
                folded = folded + square[:, n * 128 : (n + 1) * 128]
            if k == 0:
                squares[...] = folded
            else:
                squares[...] += folded

        mean_sq = jnp.sum(squares[...], axis=1, keepdims=True) * (1.0 / width)
        scale = lax.rsqrt(mean_sq + 1e-05)
        for k in range(PARTS):
            wide = pl.ds(pl.multiple_of(g * width + k * part, part), part)
            token_out = (y_acc[g, :, lanes(k)] * scale * gain_ref[:, wide]).astype(jnp.bfloat16)
            out_ref[:, wide] = token_out
            sums = dot(inside, token_out)
            own_pool[g, :, lanes(k)] = sums[:vis]
            spill_out[g, :, lanes(k)] = sums[vis:]

        @pl.when(index > 0)
        def _():
            spill_copy(g).start()

    @pl.loop(0, groups)
    def _(g):
        wide = pl.ds(pl.multiple_of(g * width, width), width)

        @pl.when(index < last_index)
        def _():
            spill_copy(g).wait_recv()
            pool_ref[:, wide] = ((own_pool[g] + spill_in[g]) / length).astype(jnp.bfloat16)

        @pl.when(index == last_index)
        def _():
            pool_ref[:, wide] = (own_pool[g] / length).astype(jnp.bfloat16)

    @pl.loop(0, chunks)
    def _(q):
        s_copy(q).wait_send()

        @pl.when(has_prev)
        def _():
            follow_copy(q).wait_send()

        @pl.when(has_next)
        def _():
            chain_copy(q).wait_send()

    @pl.when(index > 0)
    def _():
        @pl.loop(0, groups)
        def _(g):
            spill_copy(g).wait_send()

    @pl.when(index < last_index)
    def _():
        for copy in halos:
            copy.wait_send()


def ship(made_ref, pool_ref, out_ref, out_pool_ref, sems):
    copies = (
        pltpu.make_async_copy(made_ref, out_ref, sems.at[0]),
        pltpu.make_async_copy(pool_ref, out_pool_ref, sems.at[1]),
    )
    for copy in copies:
        copy.start()
    for copy in copies:
        copy.wait()


def on_device(
    x_in, bc_in, gate_z, log_decay, resets, conv_x, conv_bc, skip_d, norm_gain, visit_span
):
    tokens, channels = x_in.shape
    groups = bc_in.shape[2] // STATE
    width = PER * HEADDIM
    part = width // PARTS
    vis = visit_span.shape[0]
    chunks = PARTS * groups
    pairs = 2 * groups

    def by_group(v):
        return v.reshape(v.shape[0], 2, groups, STATE).transpose(0, 2, 1, 3).reshape(-1, STATE)

    f32, bf16 = jnp.float32, jnp.bfloat16
    state = (chunks, STATE, part)
    with_end = (chunks, STATE + 16, part)
    outside = pl.BlockSpec(memory_space=pltpu.HBM)
    inner = pl.BlockSpec(memory_space=pltpu.VMEM)
    per_chunk = pltpu.SemaphoreType.DMA((2, chunks))
    operands = (
        x_in,
        by_group(bc_in),
        gate_z,
        log_decay.transpose(0, 2, 1),
        resets[None, :],
        conv_x,
        by_group(conv_bc),
        skip_d[None, :],
        norm_gain[None, :],
        visit_span.T,
    )
    places = [pltpu.VMEM(v.shape, v.dtype) for v in operands]
    places[1] = pltpu.VMEM(((tokens + HALO) * pairs, STATE), bf16)
    made, pooled = pl.pallas_call(
        functools.partial(kernel, lax.axis_size("ctx"), groups),
        out_shape=(
            pltpu.VMEM((tokens, channels), bf16),
            pltpu.VMEM((vis, channels), bf16),
        ),
        in_specs=[outside] * 10,
        out_specs=(inner, inner),
        scratch_shapes=[
            *places,
            pltpu.VMEM((HALO, channels), bf16),
            pltpu.VMEM((2, vis), jnp.int32),
            pltpu.VMEM((tokens * pairs, STATE), f32),
            pltpu.VMEM((groups, tokens, width), bf16),
            pltpu.VMEM((groups, tokens, STATE), bf16),
            pltpu.VMEM((groups, STATE, tokens), bf16),
            pltpu.VMEM((groups, tokens, STATE), bf16),
            pltpu.VMEM((groups, tokens, 2 * PER), f32),
            pltpu.VMEM((groups, 2 * PER, tokens), f32),
            pltpu.VMEM((groups, tokens, 8 * PER), bf16),
            pltpu.VMEM((groups, 2 * PER, 128), f32),
            pltpu.VMEM((2, 8 * PER, 2 * width), bf16),
            pltpu.VMEM((tokens, 2 * width), f32),
            pltpu.VMEM((tokens, 2 * width), bf16),
            pltpu.VMEM((groups, 8, width), f32),
            pltpu.VMEM((groups, tokens, width), f32),
            pltpu.VMEM((tokens, 128), f32),
            pltpu.VMEM(state, bf16),
            pltpu.VMEM((2, *with_end), bf16),
            pltpu.VMEM(with_end, bf16),
            pltpu.VMEM(state, bf16),
            pltpu.VMEM(state, bf16),
            pltpu.VMEM(state, bf16),
            pltpu.VMEM((groups, vis, width), f32),
            pltpu.VMEM((groups, vis, width), f32),
            pltpu.VMEM((groups, vis, width), f32),
            pltpu.SemaphoreType.DMA((9,)),
            pltpu.SemaphoreType.DMA((groups,)),
            pltpu.SemaphoreType.DMA((2, 3)),
            per_chunk, per_chunk, per_chunk,
            pltpu.SemaphoreType.DMA((2, groups)),
        ],
        compiler_params=pltpu.CompilerParams(
            collective_id=0, has_side_effects=True, vmem_limit_bytes=LIMIT << 20
        ),
    )(*operands)

    return pl.pallas_call(
        ship,
        out_shape=(
            jax.ShapeDtypeStruct((tokens, channels), bf16),
            jax.ShapeDtypeStruct((vis, channels), bf16),
        ),
        in_specs=[inner, inner],
        out_specs=[pl.BlockSpec(memory_space=pl.ANY)] * 2,
        scratch_shapes=[pltpu.SemaphoreType.DMA((2,))],
        compiler_params=pltpu.CompilerParams(vmem_limit_bytes=1 << 20),
    )(pltpu.with_memory_space_constraint(made, pltpu.VMEM), pltpu.with_memory_space_constraint(pooled, pltpu.VMEM))


def solution(mesh):
    return jax.shard_map(
        on_device,
        mesh=mesh,
        in_specs=(
            P(("groups", "ctx", "dp"), "tp"),
            P(("groups", "ctx", "dp"), None, "tp"),
            P(("groups", "ctx", "dp"), "tp"),
            P(None, ("groups", "ctx", "dp"), "tp"),
            P(("groups", "ctx", "dp")),
            P(None, "tp"),
            P(None, None, "tp"),
            P("tp"),
            P("tp"),
            P(("groups", "ctx", "dp"), None),
        ),
        out_specs=(P(("groups", "ctx", "dp"), "tp"), P(("groups", "ctx", "dp"), "tp")),
        check_vma=False,
    )
```

```python
import functools
import jax
import jax.numpy as jnp
from jax import lax
from jax.experimental import pallas as pl
from jax.experimental.pallas import tpu as pltpu
from jax.sharding import PartitionSpec as P

HEADDIM = 64
STATE = 128
GROUPS = 8
PER = 16
PARTS = 4
LOG2E = 1.4426950408889634
BIG = 160.0
LIMIT = 60
HALO = 8
LAG = 2
MESH = pl.DeviceIdType.MESH


def silu(v):
    half = 0.5 * v
    return half + half * jnp.tanh(half)


def conv(padded, taps):
    total = taps[3] * padded[HALO:]
    for k in range(3):
        total = total + taps[k] * pltpu.roll(padded, 3 - k, 0)[HALO:]
    return silu(total)


def dot(a, b):
    return jnp.dot(a, b, preferred_element_type=jnp.float32)


def kernel(
    chips,
    groups,
    x_hbm, bc_hbm, gate_hbm, rate_hbm, reset_hbm, taps_x_hbm, taps_bc_hbm, skip_hbm, gain_hbm, span_hbm,
    out_ref, pool_ref,
    x_ref, bc_ref, gate_ref, rate_ref, reset_ref, taps_x, taps_bc, skip_ref, gain_ref, span_ref,
    halo_x, tail_x, tail_bc, span_in, bc_wide, xc, bs, bt, cs, colt, rowt, weights, ends, expand, spreads, sent, skips, y_acc, squares, h_lead,
    s_made, s_in, chain_in, follow_in, chain_out,
    own_pool, spill_out, spill_in,
    sem_in, sem_x, sem_halo, sem_s, sem_chain, sem_follow, sem_spill,
):
    tokens = x_ref.shape[0]
    width = PER * HEADDIM
    half = tokens // 2
    part = width // PARTS
    chunks = PARTS * groups
    pairs = 2 * groups
    c = lax.axis_index("ctx")
    d = lax.axis_index("dp")
    other = 1 - d
    nxt = c + 2 * d - 1
    prv = c - 2 * d + 1
    pos = d * c + (1 - d) * (chips - 1 - c)
    has_next = pos < chips - 1
    has_prev = pos > 0
    index = c * 2 + d
    last_index = chips * 2 - 1
    partner = {"ctx": c, "dp": other}
    halo_to = {"ctx": d * nxt + (1 - d) * c, "dp": other}
    spill_to = {"ctx": d * c + (1 - d) * nxt, "dp": other}
    follow_chain = {"ctx": nxt, "dp": d}

    barrier = pltpu.get_barrier_semaphore()

    @pl.when(has_next)
    def _():
        pl.semaphore_signal(barrier, inc=1, device_id={"ctx": nxt, "dp": other}, device_id_type=MESH)
        pl.semaphore_signal(barrier, inc=1, device_id={"ctx": nxt, "dp": d}, device_id_type=MESH)

    @pl.when(has_prev)
    def _():
        pl.semaphore_signal(barrier, inc=1, device_id={"ctx": prv, "dp": d}, device_id_type=MESH)

    pl.semaphore_signal(barrier, inc=1, device_id=partner, device_id_type=MESH)

    bc_main = bc_ref.at[pl.ds(HALO * pairs, tokens * pairs)]
    tail_rows = bc_hbm.at[pl.ds((tokens - HALO) * pairs, HALO * pairs)]
    sources = (rate_hbm, reset_hbm, bc_hbm, taps_bc_hbm, taps_x_hbm, gate_hbm, skip_hbm, gain_hbm, span_hbm,
               tail_rows, x_hbm.at[pl.ds(tokens - HALO, HALO)])
    places = (rate_ref, reset_ref, bc_main, taps_bc, taps_x, gate_ref, skip_ref, gain_ref, span_ref,
              tail_bc, tail_x)
    loads = [pltpu.make_async_copy(sources[k], places[k], sem_in.at[k]) for k in range(11)]

    def x_load(g):
        wide = pl.ds(pl.multiple_of(g * width, width), width)
        return pltpu.make_async_copy(x_hbm.at[:, wide], x_ref.at[:, wide], sem_x.at[g])

    for load in loads[9:]:
        load.start()
    for load in (*loads[:5], loads[6]):
        load.start()
    x_load(0).start()

    rows = lax.broadcasted_iota(jnp.int32, (tokens, tokens), 0)
    cols = lax.broadcasted_iota(jnp.int32, (tokens, tokens), 1)
    upto = (rows <= cols).astype(jnp.float32).astype(jnp.bfloat16)
    erow = lax.broadcasted_iota(jnp.int32, (8 * PER, width), 0)
    ehead = lax.div(lax.broadcasted_iota(jnp.int32, (8 * PER, width), 1), HEADDIM)
    for which in range(4):
        least = 4 * PER * (which // 2)
        near = lax.rem(erow, 2 * PER) == ehead + PER * (1 - which % 2)
        near = near & (erow >= least) & (erow < least + 4 * PER)
        at = (which % 2) * width
        expand[which // 2, :, at : at + width] = near.astype(jnp.float32).astype(jnp.bfloat16)

    @pl.when(pos == 0)
    def _():
        chain_in[...] = jnp.zeros_like(chain_in)

    @pl.when(pos == chips - 1)
    def _():
        follow_in[...] = jnp.zeros_like(follow_in)

    @pl.when(index == 0)
    def _():
        halo_x[...] = jnp.zeros_like(halo_x)
        bc_ref[: HALO * pairs] = jnp.zeros((HALO * pairs, STATE), jnp.bfloat16)
        span_in[...] = jnp.zeros_like(span_in)

    for load in loads[:2]:
        load.wait()

    def hi_lo(v):
        hi = v.astype(jnp.bfloat16).astype(jnp.float32)
        return jnp.concatenate([hi, v - hi], axis=0)

    fold = BIG * reset_ref[...].astype(jnp.float32)
    heads = groups * PER
    rate = jnp.concatenate([rate_ref[0], rate_ref[1]], axis=0)
    step = rate * LOG2E - fold
    step_hi = step.astype(jnp.bfloat16)
    rest = step - step_hi.astype(jnp.float32)
    step_mid = rest.astype(jnp.bfloat16)
    step_lo = (rest - step_mid.astype(jnp.float32)).astype(jnp.bfloat16)
    sums = dot(jnp.concatenate([step_hi, step_mid, step_lo], axis=0), upto)
    cum = sums[: 2 * heads] + (sums[2 * heads : 4 * heads] + sums[4 * heads :])
    is_fwd = lax.broadcasted_iota(jnp.int32, (2 * heads, tokens), 0) < heads
    r = -2.0 * rate
    small = r * (1.0 - r * (1 / 2 - r * (1 / 6 - r * (1 / 24 - r * (1 / 120 - r / 720)))))
    loss = jnp.where(r < 0.25, small, 1.0 - jnp.exp(-r))
    log_weight = jnp.maximum((0.5 * LOG2E) * jnp.log(loss), -1000.0)
    col = jnp.where(is_fwd, cum, -cum)
    row = log_weight - col
    end = cum[:, tokens - 1 : tokens]
    to_end = jnp.exp2(row + jnp.where(is_fwd, end, 0.0))
    lead = jnp.exp2(jnp.where(is_fwd, cum, end - cum))
    total = jnp.broadcast_to(jnp.exp2(end), (2 * heads, 128))

    def of_group(v, g):
        return jnp.concatenate([v[g * PER : (g + 1) * PER], v[heads + g * PER : heads + (g + 1) * PER]], axis=0)

    for g in range(groups):
        colt[g] = of_group(col, g).T
        rowt[g] = of_group(row, g)
        ends[g] = of_group(total, g)
        both = jnp.concatenate([hi_lo(of_group(to_end, g)), hi_lo(of_group(lead, g))], axis=0)
        weights[g] = both.T.astype(jnp.bfloat16)

    pl.semaphore_wait(barrier, 1 + 2 * has_next.astype(jnp.int32) + has_prev.astype(jnp.int32))

    def remote(src, dst, sems, k, to):
        return pltpu.make_async_remote_copy(
            src_ref=src, dst_ref=dst, send_sem=sems.at[0, k], recv_sem=sems.at[1, k],
            device_id=to, device_id_type=MESH,
        )

    def halo_of(g):
        wide = pl.ds(pl.multiple_of(g * width, width), width)
        return remote(tail_x.at[:, wide], halo_x.at[:, wide], sem_halo, 2 + g, halo_to)

    halo_bc = remote(tail_bc, bc_ref.at[pl.ds(0, HALO * pairs)], sem_halo, 0, halo_to)
    halo_span = remote(span_hbm, span_in, sem_halo, 1, halo_to)

    for load in loads[9:]:
        load.wait()

    @pl.when(index < last_index)
    def _():
        halo_bc.start()
        for g in range(groups):
            halo_of(g).start()
        halo_span.start()

    for g in range(1, groups):
        x_load(g).start()

    def s_copy(q):
        return remote(s_made.at[0, q], s_in.at[q], sem_s, q, partner)

    def chain_copy(q):
        return remote(chain_out.at[q], chain_in.at[q], sem_chain, q, follow_chain)

    def follow_copy(q):
        return remote(chain_in.at[q], follow_in.at[q], sem_follow, q, partner)

    def spill_copy(g):
        return remote(spill_out.at[g], spill_in.at[g], sem_spill, g, spill_to)

    for load in loads[2:5]:
        load.wait()

    def lanes(k):
        return slice(k * part, (k + 1) * part)

    def lanes_of(which, k):
        return slice(which * width + k * part, which * width + (k + 1) * part)

    def spread_end(g, which, k):
        picked = expand[0, : 2 * PER, lanes_of(which, k)].astype(jnp.float32) * ends[g, :, :1]
        return jnp.broadcast_to(jnp.sum(picked, axis=0, keepdims=True), (8, part))

    def end_of(block):
        return block[STATE : STATE + 1].astype(jnp.float32) + block[STATE + 8 : STATE + 9].astype(jnp.float32)

    def relay(q):
        s_copy(q).wait_recv()

        @pl.when(has_prev)
        def _():
            chain_copy(q).wait_recv()
            follow_copy(q).start()

        near = s_in[q]
        state = end_of(near) * chain_in[q].astype(jnp.float32) + near[:STATE].astype(jnp.float32)
        h_lead[q] = state.astype(jnp.bfloat16)

        @pl.when(has_next)
        def _():
            own = s_made[1, q]
            chain_out[q] = (end_of(own) * state + own[:STATE].astype(jnp.float32)).astype(jnp.bfloat16)
            chain_copy(q).start()

    span = 32
    per_tap = [jnp.concatenate([taps_bc[k * pairs : (k + 1) * pairs]] * (span), axis=0) for k in range(4)]

    def conv_bc(t):
        at = pl.multiple_of(t * span * pairs, span * pairs)
        raw = bc_ref[pl.ds(at, (span + HALO) * pairs)].astype(jnp.float32)
        total = per_tap[3] * raw[HALO * pairs :]
        for k in range(3):
            back = (HALO - 3 + k) * pairs
            total = total + per_tap[k] * raw[back : back + span * pairs]
        bc_wide[pl.ds(at, span * pairs)] = silu(total)

    @pl.loop(1, tokens // span)
    def _(t):
        conv_bc(t)

    def conv_x(g, above, rows_at, k):
        wide = pl.ds(pl.multiple_of(g * width + k * part, part), part)
        padded = jnp.concatenate([above, x_ref[rows_at, wide].astype(jnp.float32)], axis=0)
        made = conv(padded, [taps_x[j : j + 1, wide] for j in range(4)])
        xc[g, rows_at, lanes(k)] = made.astype(jnp.bfloat16)

    def conv_below(g):
        x_load(g).wait()
        for k in range(PARTS):
            conv_x(g, jnp.zeros((HALO, part), jnp.float32), slice(0, tokens), k)

    conv_below(0)
    loads[6].wait()

    @pl.loop(0, groups)
    def _(g):
        at = lax.broadcasted_iota(jnp.int32, (groups * PER, width), 0)
        head = lax.div(lax.broadcasted_iota(jnp.int32, (groups * PER, width), 1), HEADDIM)
        pick = (at == head + g * PER).astype(jnp.float32)
        skips[g] = lax.dot(jnp.broadcast_to(skip_ref[...], (8, groups * PER)), pick,
                           precision=lax.Precision.HIGHEST, preferred_element_type=jnp.float32)

    @pl.when(index > 0)
    def _():
        halo_bc.wait_recv()

    conv_bc(0)
    for load in (loads[5], *loads[7:9]):
        load.start()

    for g in range(groups):
        b_g = bc_wide[pl.ds(2 * g, tokens, stride=pairs), :]
        bs[g] = b_g.astype(jnp.bfloat16)
        bt[g] = b_g.T.astype(jnp.bfloat16)
        cs[g] = bc_wide[pl.ds(2 * g + 1, tokens, stride=pairs), :].astype(jnp.bfloat16)

    early = jnp.where(d == 0, 870 + 300 * (pos - 1), 850 + 300 * (pos - 1))

    def due_at(time):
        return jnp.clip(lax.div(time - early + 7800, 78) - 99, 0, chunks)

    def due_first(g):
        return jnp.where(pos == 0, jnp.clip(g * PARTS + PARTS - LAG, 0, chunks), due_at(1050 - 140 * (groups - 1 - g)))

    def due(unit):
        return jnp.where(pos == 0, chunks, due_at(1050 + 47 * unit))

    @pl.loop(0, groups)
    def _(g):
        spreads[...] = dot(weights[g], expand[0])

        @pl.when(index > 0)
        def _():
            halo_of(g).wait_recv()

        for k in range(PARTS):
            wide = pl.ds(pl.multiple_of(g * width + k * part, part), part)
            conv_x(g, halo_x[:, wide].astype(jnp.float32), slice(0, 16), k)
            xf = xc[g, :, lanes(k)].astype(jnp.float32)
            for which in range(2):
                sent[:, lanes_of(which, k)] = (xf * spreads[:, lanes_of(which, k)]).astype(jnp.bfloat16)
        made = dot(bt[g], sent[...]).astype(jnp.bfloat16)
        for k in range(PARTS):
            q = g * PARTS + k
            for which in range(2):
                role = d if which == 0 else other
                s_made[1 - role, q, :STATE] = made[:, lanes_of(which, k)]
                s_made[1 - role, q, STATE:] = hi_lo(spread_end(g, which, k)).astype(jnp.bfloat16)
            s_copy(q).start()

        @pl.loop(jnp.where(g == 0, 0, due_first(g - 1)), due_first(g))
        def _(q):
            relay(q)

        @pl.when(g < groups - 1)
        def _():
            conv_below(g + 1)

    @pl.when(pos == 0)
    def _():
        @pl.loop(max(chunks - LAG, 0), chunks)
        def _(q):
            relay(q)

    left = lax.broadcasted_iota(jnp.int32, (tokens, 128), 1) < HEADDIM
    lower = rows[:half, :half] >= cols[:half, :half]

    @pl.loop(0, groups)
    def _(g):
        score = lax.dot_general(cs[g], bs[g], (((1,), (1,)), ((), ())), preferred_element_type=jnp.float32)
        for quarter in range(4):
            unit = 4 * g + quarter
            @pl.loop(jnp.where(unit == 0, jnp.where(pos == 0, chunks, due_first(groups - 1)), due(unit - 1)), due(unit))
            def _(q):
                relay(q)

            for pair in range(quarter * PER // 8, (quarter + 1) * PER // 8):
                at = pair * 2 * HEADDIM
                x_pair = xc[g, :, at : at + 2 * HEADDIM]
                got = []
                for head in (2 * pair, 2 * pair + 1):
                    cf = colt[g, :, head : head + 1]
                    cb = colt[g, :, PER + head : PER + head + 1]
                    rf = rowt[g, head : head + 1, :]
                    rb = rowt[g, PER + head : PER + head + 1, :]
                    tl = jnp.where(lower, cf[:half] + rf[:, :half], cb[:half] + rb[:, :half])
                    tr = cb[:half] + rb[:, half:]
                    bl = cf[half:] + rf[:, :half]
                    br = jnp.where(lower, cf[half:] + rf[:, half:], cb[half:] + rb[:, half:])
                    top = jnp.concatenate([tl, tr], axis=1)
                    bottom = jnp.concatenate([bl, br], axis=1)
                    mix_top = (score[:half] * jnp.exp2(top)).astype(jnp.bfloat16)
                    mix_bottom = (score[half:] * jnp.exp2(bottom)).astype(jnp.bfloat16)
                    got.append(dot(jnp.concatenate([mix_top, mix_bottom], axis=0), x_pair))
                y_acc[g, :, at : at + 2 * HEADDIM] = jnp.where(left, got[0], got[1])

    for load in (loads[5], *loads[7:9]):
        load.wait()

    @pl.when(index > 0)
    def _():
        halo_span.wait_recv()

    vis = span_ref.shape[1]
    token = index * tokens + lax.broadcasted_iota(jnp.int32, (tokens, vis), 0)

    def covers(ref):
        return ((token >= ref[0:1]) & (token < ref[1:2])).astype(jnp.float32).T

    inside = jnp.concatenate([covers(span_ref), covers(span_in)], axis=0).astype(jnp.bfloat16)
    same = lax.broadcasted_iota(jnp.int32, (vis, vis), 0) == lax.broadcasted_iota(jnp.int32, (vis, vis), 1)
    spanned = jnp.maximum(span_ref[1:2] - span_ref[0:1], 1).astype(jnp.float32)
    length = jnp.sum(jnp.where(same, spanned, 0.0), axis=1, keepdims=True)

    before = due(4 * groups - 1)

    def reached(step):
        further = before + lax.div(step, 1) + 1
        return jnp.clip(jnp.maximum(step + 1, jnp.where(has_next, further, before)), 0, chunks)

    def all_sent(g):
        for k in range(PARTS):
            q = g * PARTS + k
            s_copy(q).wait_send()

            @pl.when(has_prev)
            def _():
                follow_copy(q).wait_send()

            @pl.when(has_next)
            def _():
                chain_copy(q).wait_send()

    @pl.loop(0, groups)
    def _(g):
        @pl.when(g > 0)
        def _():
            all_sent(g - 1)

        spreads[...] = dot(weights[g], expand[1])
        for k in range(PARTS // 2):
            q = g * PARTS + 2 * k

            @pl.loop(jnp.where(q == 0, before, reached(q - 1)), reached(q + 1))
            def _(p):
                relay(p)

            @pl.when(has_next)
            def _():
                follow_copy(q).wait_recv()
                follow_copy(q + 1).wait_recv()

            wide = pl.ds(pl.multiple_of(g * width + 2 * k * part, part), 2 * part)
            near = pl.ds(pl.multiple_of(d * width + 2 * k * part, part), 2 * part)
            far = pl.ds(pl.multiple_of(other * width + 2 * k * part, part), 2 * part)
            here = slice(2 * k * part, (2 * k + 2) * part)
            c_g = cs[g]
            lead = spreads[:, near] * dot(c_g, jnp.concatenate([h_lead[q], h_lead[q + 1]], axis=1))
            lead = lead + spreads[:, far] * dot(c_g, jnp.concatenate([follow_in[q], follow_in[q + 1]], axis=1))
            mixed = y_acc[g, :, here] + lead + skips[g, 0:1, here] * xc[g, :, here].astype(jnp.float32)
            gated = mixed * silu(gate_ref[:, wide].astype(jnp.float32))
            y_acc[g, :, here] = gated
            square = gated * gated
            folded = square[:, :128]
            for n in range(1, part // 64):
                folded = folded + square[:, n * 128 : (n + 1) * 128]
            if k == 0:
                squares[...] = folded
            else:
                squares[...] += folded

        mean_sq = jnp.sum(squares[...], axis=1, keepdims=True) * (1.0 / width)
        scale = lax.rsqrt(mean_sq + 1e-05)
        for k in range(PARTS):
            wide = pl.ds(pl.multiple_of(g * width + k * part, part), part)
            token_out = (y_acc[g, :, lanes(k)] * scale * gain_ref[:, wide]).astype(jnp.bfloat16)
            out_ref[:, wide] = token_out
            sums = dot(inside, token_out)
            own_pool[g, :, lanes(k)] = sums[:vis]
            spill_out[g, :, lanes(k)] = sums[vis:]

        @pl.when(index > 0)
        def _():
            spill_copy(g).start()

    @pl.loop(0, groups)
    def _(g):
        wide = pl.ds(pl.multiple_of(g * width, width), width)

        @pl.when(index < last_index)
        def _():
            spill_copy(g).wait_recv()
            pool_ref[:, wide] = ((own_pool[g] + spill_in[g]) / length).astype(jnp.bfloat16)

        @pl.when(index == last_index)
        def _():
            pool_ref[:, wide] = (own_pool[g] / length).astype(jnp.bfloat16)

    all_sent(groups - 1)

    @pl.when(index > 0)
    def _():
        @pl.loop(0, groups)
        def _(g):
            spill_copy(g).wait_send()

    @pl.when(index < last_index)
    def _():
        halo_bc.wait_send()
        halo_span.wait_send()
        for g in range(groups):
            halo_of(g).wait_send()


def ship(made_ref, pool_ref, out_ref, out_pool_ref, sems):
    copies = (
        pltpu.make_async_copy(made_ref, out_ref, sems.at[0]),
        pltpu.make_async_copy(pool_ref, out_pool_ref, sems.at[1]),
    )
    for copy in copies:
        copy.start()
    for copy in copies:
        copy.wait()


def on_device(
    x_in, bc_in, gate_z, log_decay, resets, conv_x, conv_bc, skip_d, norm_gain, visit_span
):
    tokens, channels = x_in.shape
    groups = bc_in.shape[2] // STATE
    width = PER * HEADDIM
    part = width // PARTS
    vis = visit_span.shape[0]
    chunks = PARTS * groups
    pairs = 2 * groups

    def by_group(v):
        return v.reshape(v.shape[0], 2, groups, STATE).transpose(0, 2, 1, 3).reshape(-1, STATE)

    f32, bf16 = jnp.float32, jnp.bfloat16
    state = (chunks, STATE, part)
    with_end = (chunks, STATE + 16, part)
    outside = pl.BlockSpec(memory_space=pltpu.HBM)
    inner = pl.BlockSpec(memory_space=pltpu.VMEM)
    per_chunk = pltpu.SemaphoreType.DMA((2, chunks))
    operands = (
        x_in,
        by_group(bc_in),
        gate_z,
        log_decay.transpose(0, 2, 1),
        resets[None, :],
        conv_x,
        by_group(conv_bc),
        skip_d[None, :],
        norm_gain[None, :],
        visit_span.T,
    )
    places = [pltpu.VMEM(v.shape, v.dtype) for v in operands]
    places[1] = pltpu.VMEM(((tokens + HALO) * pairs, STATE), bf16)
    made, pooled = pl.pallas_call(
        functools.partial(kernel, lax.axis_size("ctx"), groups),
        out_shape=(
            pltpu.VMEM((tokens, channels), bf16),
            pltpu.VMEM((vis, channels), bf16),
        ),
        in_specs=[outside] * 10,
        out_specs=(inner, inner),
        scratch_shapes=[
            *places,
            pltpu.VMEM((HALO, channels), bf16),
            pltpu.VMEM((HALO, channels), bf16),
            pltpu.VMEM((HALO * pairs, STATE), bf16),
            pltpu.VMEM((2, vis), jnp.int32),
            pltpu.VMEM((tokens * pairs, STATE), f32),
            pltpu.VMEM((groups, tokens, width), bf16),
            pltpu.VMEM((groups, tokens, STATE), bf16),
            pltpu.VMEM((groups, STATE, tokens), bf16),
            pltpu.VMEM((groups, tokens, STATE), bf16),
            pltpu.VMEM((groups, tokens, 2 * PER), f32),
            pltpu.VMEM((groups, 2 * PER, tokens), f32),
            pltpu.VMEM((groups, tokens, 8 * PER), bf16),
            pltpu.VMEM((groups, 2 * PER, 128), f32),
            pltpu.VMEM((2, 8 * PER, 2 * width), bf16),
            pltpu.VMEM((tokens, 2 * width), f32),
            pltpu.VMEM((tokens, 2 * width), bf16),
            pltpu.VMEM((groups, 8, width), f32),
            pltpu.VMEM((groups, tokens, width), f32),
            pltpu.VMEM((tokens, 128), f32),
            pltpu.VMEM(state, bf16),
            pltpu.VMEM((2, *with_end), bf16),
            pltpu.VMEM(with_end, bf16),
            pltpu.VMEM(state, bf16),
            pltpu.VMEM(state, bf16),
            pltpu.VMEM(state, bf16),
            pltpu.VMEM((groups, vis, width), f32),
            pltpu.VMEM((groups, vis, width), f32),
            pltpu.VMEM((groups, vis, width), f32),
            pltpu.SemaphoreType.DMA((11,)),
            pltpu.SemaphoreType.DMA((groups,)),
            pltpu.SemaphoreType.DMA((2, 2 + groups)),
            per_chunk, per_chunk, per_chunk,
            pltpu.SemaphoreType.DMA((2, groups)),
        ],
        compiler_params=pltpu.CompilerParams(
            collective_id=0, has_side_effects=True, vmem_limit_bytes=LIMIT << 20
        ),
    )(*operands)

    return pl.pallas_call(
        ship,
        out_shape=(
            jax.ShapeDtypeStruct((tokens, channels), bf16),
            jax.ShapeDtypeStruct((vis, channels), bf16),
        ),
        in_specs=[inner, inner],
        out_specs=[pl.BlockSpec(memory_space=pl.ANY)] * 2,
        scratch_shapes=[pltpu.SemaphoreType.DMA((2,))],
        compiler_params=pltpu.CompilerParams(vmem_limit_bytes=1 << 20),
    )(pltpu.with_memory_space_constraint(made, pltpu.VMEM), pltpu.with_memory_space_constraint(pooled, pltpu.VMEM))


def solution(mesh):
    return jax.shard_map(
        on_device,
        mesh=mesh,
        in_specs=(
            P(("groups", "ctx", "dp"), "tp"),
            P(("groups", "ctx", "dp"), None, "tp"),
            P(("groups", "ctx", "dp"), "tp"),
            P(None, ("groups", "ctx", "dp"), "tp"),
            P(("groups", "ctx", "dp")),
            P(None, "tp"),
            P(None, None, "tp"),
            P("tp"),
            P("tp"),
            P(("groups", "ctx", "dp"), None),
        ),
        out_specs=(P(("groups", "ctx", "dp"), "tp"), P(("groups", "ctx", "dp"), "tp")),
        check_vma=False,
    )
```

```python
import functools
import jax
import jax.numpy as jnp
from jax import lax
from jax.experimental import pallas as pl
from jax.experimental.pallas import tpu as pltpu
from jax.sharding import PartitionSpec as P

HEADDIM = 64
STATE = 128
GROUPS = 8
PER = 16
PARTS = 4
LOG2E = 1.4426950408889634
BIG = 160.0
LIMIT = 60
HALO = 8
LAG = 2
MESH = pl.DeviceIdType.MESH


def silu(v):
    half = 0.5 * v
    return half + half * jnp.tanh(half)


def conv(padded, taps):
    total = taps[3] * padded[HALO:]
    for k in range(3):
        total = total + taps[k] * pltpu.roll(padded, 3 - k, 0)[HALO:]
    return silu(total)


def dot(a, b):
    return jnp.dot(a, b, preferred_element_type=jnp.float32)


def kernel(
    chips,
    groups,
    x_hbm, bc_hbm, gate_hbm, rate_hbm, reset_hbm, taps_x_hbm, taps_bc_hbm, skip_hbm, gain_hbm, span_hbm,
    out_ref, pool_ref,
    x_ref, bc_ref, gate_ref, rate_ref, reset_ref, taps_x, taps_bc, skip_ref, gain_ref, span_ref,
    halo_x, tail_x, tail_bc, span_in, bc_wide, xc, bs, bt, cs, colt, rowt, weights, ends, expand, spreads, sent, shifted, skips, y_acc, squares, h_lead,
    s_made, s_in, chain_in, follow_in, chain_out,
    own_pool, spill_out, spill_in,
    sem_in, sem_x, sem_halo, sem_s, sem_chain, sem_follow, sem_spill,
):
    tokens = x_ref.shape[0]
    width = PER * HEADDIM
    half = tokens // 2
    part = width // PARTS
    chunks = PARTS * groups
    pairs = 2 * groups
    c = lax.axis_index("ctx")
    d = lax.axis_index("dp")
    other = 1 - d
    nxt = c + 2 * d - 1
    prv = c - 2 * d + 1
    pos = d * c + (1 - d) * (chips - 1 - c)
    has_next = pos < chips - 1
    has_prev = pos > 0
    index = c * 2 + d
    last_index = chips * 2 - 1
    partner = {"ctx": c, "dp": other}
    halo_to = {"ctx": d * nxt + (1 - d) * c, "dp": other}
    spill_to = {"ctx": d * c + (1 - d) * nxt, "dp": other}
    follow_chain = {"ctx": nxt, "dp": d}

    barrier = pltpu.get_barrier_semaphore()

    @pl.when(has_next)
    def _():
        pl.semaphore_signal(barrier, inc=1, device_id={"ctx": nxt, "dp": other}, device_id_type=MESH)
        pl.semaphore_signal(barrier, inc=1, device_id={"ctx": nxt, "dp": d}, device_id_type=MESH)

    @pl.when(has_prev)
    def _():
        pl.semaphore_signal(barrier, inc=1, device_id={"ctx": prv, "dp": d}, device_id_type=MESH)

    pl.semaphore_signal(barrier, inc=1, device_id=partner, device_id_type=MESH)

    bc_main = bc_ref.at[pl.ds(HALO * pairs, tokens * pairs)]
    tail_rows = bc_hbm.at[pl.ds((tokens - HALO) * pairs, HALO * pairs)]
    sources = (rate_hbm, reset_hbm, bc_hbm, taps_bc_hbm, taps_x_hbm, gate_hbm, skip_hbm, gain_hbm, span_hbm,
               tail_rows, x_hbm.at[pl.ds(tokens - HALO, HALO)])
    places = (rate_ref, reset_ref, bc_main, taps_bc, taps_x, gate_ref, skip_ref, gain_ref, span_ref,
              tail_bc, tail_x)
    loads = [pltpu.make_async_copy(sources[k], places[k], sem_in.at[k]) for k in range(11)]

    def x_load(g):
        wide = pl.ds(pl.multiple_of(g * width, width), width)
        return pltpu.make_async_copy(x_hbm.at[:, wide], x_ref.at[:, wide], sem_x.at[g])

    for load in loads[9:]:
        load.start()
    for load in (*loads[:5], loads[6]):
        load.start()
    x_load(0).start()

    rows = lax.broadcasted_iota(jnp.int32, (tokens, tokens), 0)
    cols = lax.broadcasted_iota(jnp.int32, (tokens, tokens), 1)
    upto = (rows <= cols).astype(jnp.float32).astype(jnp.bfloat16)
    erow = lax.broadcasted_iota(jnp.int32, (8 * PER, width), 0)
    ehead = lax.div(lax.broadcasted_iota(jnp.int32, (8 * PER, width), 1), HEADDIM)
    for which in range(4):
        least = 4 * PER * (which // 2)
        near = lax.rem(erow, 2 * PER) == ehead + PER * (1 - which % 2)
        near = near & (erow >= least) & (erow < least + 4 * PER)
        at = (which % 2) * width
        expand[which // 2, :, at : at + width] = near.astype(jnp.float32).astype(jnp.bfloat16)

    shifted[:, :HALO, :] = jnp.zeros((4, HALO, 128), jnp.float32)

    @pl.when(pos == 0)
    def _():
        chain_in[...] = jnp.zeros_like(chain_in)

    @pl.when(pos == chips - 1)
    def _():
        follow_in[...] = jnp.zeros_like(follow_in)

    @pl.when(index == 0)
    def _():
        halo_x[...] = jnp.zeros_like(halo_x)
        bc_ref[: HALO * pairs] = jnp.zeros((HALO * pairs, STATE), jnp.bfloat16)
        span_in[...] = jnp.zeros_like(span_in)

    for load in loads[:2]:
        load.wait()

    def hi_lo(v):
        hi = v.astype(jnp.bfloat16).astype(jnp.float32)
        return jnp.concatenate([hi, v - hi], axis=0)

    fold = BIG * reset_ref[...].astype(jnp.float32)
    heads = groups * PER
    rate = jnp.concatenate([rate_ref[0], rate_ref[1]], axis=0)
    step = rate * LOG2E - fold
    step_hi = step.astype(jnp.bfloat16)
    rest = step - step_hi.astype(jnp.float32)
    step_mid = rest.astype(jnp.bfloat16)
    step_lo = (rest - step_mid.astype(jnp.float32)).astype(jnp.bfloat16)
    sums = dot(jnp.concatenate([step_hi, step_mid, step_lo], axis=0), upto)
    cum = sums[: 2 * heads] + (sums[2 * heads : 4 * heads] + sums[4 * heads :])
    is_fwd = lax.broadcasted_iota(jnp.int32, (2 * heads, tokens), 0) < heads
    r = -2.0 * rate
    small = r * (1.0 - r * (1 / 2 - r * (1 / 6 - r * (1 / 24 - r * (1 / 120 - r / 720)))))
    loss = jnp.where(r < 0.25, small, 1.0 - jnp.exp(-r))
    log_weight = jnp.maximum((0.5 * LOG2E) * jnp.log(loss), -1000.0)
    col = jnp.where(is_fwd, cum, -cum)
    row = log_weight - col
    end = cum[:, tokens - 1 : tokens]
    to_end = jnp.exp2(row + jnp.where(is_fwd, end, 0.0))
    lead = jnp.exp2(jnp.where(is_fwd, cum, end - cum))
    total = jnp.broadcast_to(jnp.exp2(end), (2 * heads, 128))

    def of_group(v, g):
        return jnp.concatenate([v[g * PER : (g + 1) * PER], v[heads + g * PER : heads + (g + 1) * PER]], axis=0)

    for g in range(groups):
        colt[g] = of_group(col, g).T
        rowt[g] = of_group(row, g)
        ends[g] = of_group(total, g)
        both = jnp.concatenate([hi_lo(of_group(to_end, g)), hi_lo(of_group(lead, g))], axis=0)
        weights[g] = both.T.astype(jnp.bfloat16)

    pl.semaphore_wait(barrier, 1 + 2 * has_next.astype(jnp.int32) + has_prev.astype(jnp.int32))

    def remote(src, dst, sems, k, to):
        return pltpu.make_async_remote_copy(
            src_ref=src, dst_ref=dst, send_sem=sems.at[0, k], recv_sem=sems.at[1, k],
            device_id=to, device_id_type=MESH,
        )

    def halo_of(g):
        wide = pl.ds(pl.multiple_of(g * width, width), width)
        return remote(tail_x.at[:, wide], halo_x.at[:, wide], sem_halo, 2 + g, halo_to)

    halo_bc = remote(tail_bc, bc_ref.at[pl.ds(0, HALO * pairs)], sem_halo, 0, halo_to)
    halo_span = remote(span_hbm, span_in, sem_halo, 1, halo_to)

    for load in loads[9:]:
        load.wait()

    @pl.when(index < last_index)
    def _():
        halo_bc.start()
        for g in range(groups):
            halo_of(g).start()
        halo_span.start()

    for g in range(1, groups):
        x_load(g).start()

    def s_copy(q):
        return remote(s_made.at[0, q], s_in.at[q], sem_s, q, partner)

    def chain_copy(q):
        return remote(chain_out.at[q], chain_in.at[q], sem_chain, q, follow_chain)

    def follow_copy(q):
        return remote(chain_in.at[q], follow_in.at[q], sem_follow, q, partner)

    def spill_copy(g):
        return remote(spill_out.at[g], spill_in.at[g], sem_spill, g, spill_to)

    for load in loads[2:5]:
        load.wait()

    def lanes(k):
        return slice(k * part, (k + 1) * part)

    def lanes_of(which, k):
        return slice(which * width + k * part, which * width + (k + 1) * part)

    def spread_end(g, which, k):
        picked = expand[0, : 2 * PER, lanes_of(which, k)].astype(jnp.float32) * ends[g, :, :1]
        return jnp.broadcast_to(jnp.sum(picked, axis=0, keepdims=True), (8, part))

    def end_of(block):
        return block[STATE : STATE + 1].astype(jnp.float32) + block[STATE + 8 : STATE + 9].astype(jnp.float32)

    def relay(q):
        s_copy(q).wait_recv()

        @pl.when(has_prev)
        def _():
            chain_copy(q).wait_recv()
            follow_copy(q).start()

        near = s_in[q]
        state = end_of(near) * chain_in[q].astype(jnp.float32) + near[:STATE].astype(jnp.float32)
        h_lead[q] = state.astype(jnp.bfloat16)

        @pl.when(has_next)
        def _():
            own = s_made[1, q]
            chain_out[q] = (end_of(own) * state + own[:STATE].astype(jnp.float32)).astype(jnp.bfloat16)
            chain_copy(q).start()

    span = 32
    per_tap = [jnp.concatenate([taps_bc[k * pairs : (k + 1) * pairs]] * (span), axis=0) for k in range(4)]

    def conv_bc(t):
        at = pl.multiple_of(t * span * pairs, span * pairs)
        raw = bc_ref[pl.ds(at, (span + HALO) * pairs)].astype(jnp.float32)
        total = per_tap[3] * raw[HALO * pairs :]
        for k in range(3):
            back = (HALO - 3 + k) * pairs
            total = total + per_tap[k] * raw[back : back + span * pairs]
        bc_wide[pl.ds(at, span * pairs)] = silu(total)

    @pl.loop(1, tokens // span)
    def _(t):
        conv_bc(t)

    def conv_x(g, above, rows_at, k):
        wide = pl.ds(pl.multiple_of(g * width + k * part, part), part)
        padded = jnp.concatenate([above, x_ref[rows_at, wide].astype(jnp.float32)], axis=0)
        made = conv(padded, [taps_x[j : j + 1, wide] for j in range(4)])
        xc[g, rows_at, lanes(k)] = made.astype(jnp.bfloat16)

    def conv_below(g):
        x_load(g).wait()
        for k in range(width // 128):
            wide = pl.ds(pl.multiple_of(g * width + k * 128, 128), 128)
            slot = k % 4
            shifted[slot, HALO:, :] = x_ref[:, wide].astype(jnp.float32)
            total = taps_x[3:4, wide] * shifted[slot, HALO:, :]
            for j in range(3):
                total = total + taps_x[j : j + 1, wide] * shifted[slot, HALO - 3 + j : HALO - 3 + j + tokens, :]
            xc[g, :, k * 128 : (k + 1) * 128] = silu(total).astype(jnp.bfloat16)

    conv_below(0)
    loads[6].wait()

    @pl.loop(0, groups)
    def _(g):
        at = lax.broadcasted_iota(jnp.int32, (groups * PER, width), 0)
        head = lax.div(lax.broadcasted_iota(jnp.int32, (groups * PER, width), 1), HEADDIM)
        pick = (at == head + g * PER).astype(jnp.float32)
        skips[g] = lax.dot(jnp.broadcast_to(skip_ref[...], (8, groups * PER)), pick,
                           precision=lax.Precision.HIGHEST, preferred_element_type=jnp.float32)

    @pl.when(index > 0)
    def _():
        halo_bc.wait_recv()

    conv_bc(0)
    for load in (loads[5], *loads[7:9]):
        load.start()

    for g in range(groups):
        b_g = bc_wide[pl.ds(2 * g, tokens, stride=pairs), :]
        bs[g] = b_g.astype(jnp.bfloat16)
        bt[g] = b_g.T.astype(jnp.bfloat16)
        cs[g] = bc_wide[pl.ds(2 * g + 1, tokens, stride=pairs), :].astype(jnp.bfloat16)

    early = jnp.where(d == 0, 870 + 300 * (pos - 1), 850 + 300 * (pos - 1))

    def due_at(time):
        return jnp.clip(lax.div(time - early + 7800, 78) - 99, 0, chunks)

    def due_first(g):
        return jnp.where(pos == 0, jnp.clip(g * PARTS + PARTS - LAG, 0, chunks), due_at(1050 - 140 * (groups - 1 - g)))

    def due(unit):
        return jnp.where(pos == 0, chunks, due_at(1050 + 47 * unit))

    @pl.loop(0, groups)
    def _(g):
        spreads[...] = dot(weights[g], expand[0])

        @pl.when(index > 0)
        def _():
            halo_of(g).wait_recv()

        for k in range(PARTS):
            wide = pl.ds(pl.multiple_of(g * width + k * part, part), part)
            conv_x(g, halo_x[:, wide].astype(jnp.float32), slice(0, 16), k)
            xf = xc[g, :, lanes(k)].astype(jnp.float32)
            for which in range(2):
                sent[:, lanes_of(which, k)] = (xf * spreads[:, lanes_of(which, k)]).astype(jnp.bfloat16)
        made = dot(bt[g], sent[...]).astype(jnp.bfloat16)
        for k in range(PARTS):
            q = g * PARTS + k
            for which in range(2):
                role = d if which == 0 else other
                s_made[1 - role, q, :STATE] = made[:, lanes_of(which, k)]
                s_made[1 - role, q, STATE:] = hi_lo(spread_end(g, which, k)).astype(jnp.bfloat16)
            s_copy(q).start()

        @pl.loop(jnp.where(g == 0, 0, due_first(g - 1)), due_first(g))
        def _(q):
            relay(q)

        @pl.when(g < groups - 1)
        def _():
            conv_below(g + 1)

    @pl.when(pos == 0)
    def _():
        @pl.loop(max(chunks - LAG, 0), chunks)
        def _(q):
            relay(q)

    left = lax.broadcasted_iota(jnp.int32, (tokens, 128), 1) < HEADDIM
    lower = rows[:half, :half] >= cols[:half, :half]

    @pl.loop(0, groups)
    def _(g):
        score = lax.dot_general(cs[g], bs[g], (((1,), (1,)), ((), ())), preferred_element_type=jnp.float32)
        for quarter in range(2):
            unit = 4 * g + 2 * quarter + 1
            @pl.loop(jnp.where(unit == 1, jnp.where(pos == 0, chunks, due_first(groups - 1)), due(unit - 2)), due(unit))
            def _(q):
                relay(q)

            for pair in range(quarter * PER // 4, (quarter + 1) * PER // 4):
                at = pair * 2 * HEADDIM
                x_pair = xc[g, :, at : at + 2 * HEADDIM]
                got = []
                for head in (2 * pair, 2 * pair + 1):
                    cf = colt[g, :, head : head + 1]
                    cb = colt[g, :, PER + head : PER + head + 1]
                    rf = rowt[g, head : head + 1, :]
                    rb = rowt[g, PER + head : PER + head + 1, :]
                    tl = jnp.where(lower, cf[:half] + rf[:, :half], cb[:half] + rb[:, :half])
                    tr = cb[:half] + rb[:, half:]
                    bl = cf[half:] + rf[:, :half]
                    br = jnp.where(lower, cf[half:] + rf[:, half:], cb[half:] + rb[:, half:])
                    top = jnp.concatenate([tl, tr], axis=1)
                    bottom = jnp.concatenate([bl, br], axis=1)
                    mix_top = (score[:half] * jnp.exp2(top)).astype(jnp.bfloat16)
                    mix_bottom = (score[half:] * jnp.exp2(bottom)).astype(jnp.bfloat16)
                    got.append(dot(jnp.concatenate([mix_top, mix_bottom], axis=0), x_pair))
                y_acc[g, :, at : at + 2 * HEADDIM] = jnp.where(left, got[0], got[1])

    for load in (loads[5], *loads[7:9]):
        load.wait()

    @pl.when(index > 0)
    def _():
        halo_span.wait_recv()

    vis = span_ref.shape[1]
    token = index * tokens + lax.broadcasted_iota(jnp.int32, (tokens, vis), 0)

    def covers(ref):
        return ((token >= ref[0:1]) & (token < ref[1:2])).astype(jnp.float32).T

    inside = jnp.concatenate([covers(span_ref), covers(span_in)], axis=0).astype(jnp.bfloat16)
    same = lax.broadcasted_iota(jnp.int32, (vis, vis), 0) == lax.broadcasted_iota(jnp.int32, (vis, vis), 1)
    spanned = jnp.maximum(span_ref[1:2] - span_ref[0:1], 1).astype(jnp.float32)
    length = jnp.sum(jnp.where(same, spanned, 0.0), axis=1, keepdims=True)

    before = due(4 * groups - 1)

    def reached(step):
        further = before + lax.div(step, 1) + 1
        return jnp.clip(jnp.maximum(step + 1, jnp.where(has_next, further, before)), 0, chunks)

    def all_sent(g):
        for k in range(PARTS):
            q = g * PARTS + k
            s_copy(q).wait_send()

            @pl.when(has_prev)
            def _():
                follow_copy(q).wait_send()

            @pl.when(has_next)
            def _():
                chain_copy(q).wait_send()

    @pl.loop(0, groups)
    def _(g):
        @pl.when(g > 0)
        def _():
            all_sent(g - 1)

        spreads[...] = dot(weights[g], expand[1])
        for k in range(PARTS // 2):
            q = g * PARTS + 2 * k

            @pl.loop(jnp.where(q == 0, before, reached(q - 1)), reached(q + 1))
            def _(p):
                relay(p)

            @pl.when(has_next)
            def _():
                follow_copy(q).wait_recv()
                follow_copy(q + 1).wait_recv()

            wide = pl.ds(pl.multiple_of(g * width + 2 * k * part, part), 2 * part)
            near = pl.ds(pl.multiple_of(d * width + 2 * k * part, part), 2 * part)
            far = pl.ds(pl.multiple_of(other * width + 2 * k * part, part), 2 * part)
            here = slice(2 * k * part, (2 * k + 2) * part)
            c_g = cs[g]
            lead = spreads[:, near] * dot(c_g, jnp.concatenate([h_lead[q], h_lead[q + 1]], axis=1))
            lead = lead + spreads[:, far] * dot(c_g, jnp.concatenate([follow_in[q], follow_in[q + 1]], axis=1))
            mixed = y_acc[g, :, here] + lead + skips[g, 0:1, here] * xc[g, :, here].astype(jnp.float32)
            gated = mixed * silu(gate_ref[:, wide].astype(jnp.float32))
            y_acc[g, :, here] = gated
            square = gated * gated
            folded = square[:, :128]
            for n in range(1, part // 64):
                folded = folded + square[:, n * 128 : (n + 1) * 128]
            if k == 0:
                squares[...] = folded
            else:
                squares[...] += folded

        mean_sq = jnp.sum(squares[...], axis=1, keepdims=True) * (1.0 / width)
        scale = lax.rsqrt(mean_sq + 1e-05)
        for k in range(PARTS):
            wide = pl.ds(pl.multiple_of(g * width + k * part, part), part)
            token_out = (y_acc[g, :, lanes(k)] * scale * gain_ref[:, wide]).astype(jnp.bfloat16)
            out_ref[:, wide] = token_out
            sums = dot(inside, token_out)
            own_pool[g, :, lanes(k)] = sums[:vis]
            spill_out[g, :, lanes(k)] = sums[vis:]

        @pl.when(index > 0)
        def _():
            spill_copy(g).start()

    @pl.loop(0, groups)
    def _(g):
        wide = pl.ds(pl.multiple_of(g * width, width), width)

        @pl.when(index < last_index)
        def _():
            spill_copy(g).wait_recv()
            pool_ref[:, wide] = ((own_pool[g] + spill_in[g]) / length).astype(jnp.bfloat16)

        @pl.when(index == last_index)
        def _():
            pool_ref[:, wide] = (own_pool[g] / length).astype(jnp.bfloat16)

    all_sent(groups - 1)

    @pl.when(index > 0)
    def _():
        @pl.loop(0, groups)
        def _(g):
            spill_copy(g).wait_send()

    @pl.when(index < last_index)
    def _():
        halo_bc.wait_send()
        halo_span.wait_send()
        for g in range(groups):
            halo_of(g).wait_send()


def ship(made_ref, pool_ref, out_ref, out_pool_ref, sems):
    copies = (
        pltpu.make_async_copy(made_ref, out_ref, sems.at[0]),
        pltpu.make_async_copy(pool_ref, out_pool_ref, sems.at[1]),
    )
    for copy in copies:
        copy.start()
    for copy in copies:
        copy.wait()


def on_device(
    x_in, bc_in, gate_z, log_decay, resets, conv_x, conv_bc, skip_d, norm_gain, visit_span
):
    tokens, channels = x_in.shape
    groups = bc_in.shape[2] // STATE
    width = PER * HEADDIM
    part = width // PARTS
    vis = visit_span.shape[0]
    chunks = PARTS * groups
    pairs = 2 * groups

    def by_group(v):
        return v.reshape(v.shape[0], 2, groups, STATE).transpose(0, 2, 1, 3).reshape(-1, STATE)

    f32, bf16 = jnp.float32, jnp.bfloat16
    state = (chunks, STATE, part)
    with_end = (chunks, STATE + 16, part)
    outside = pl.BlockSpec(memory_space=pltpu.HBM)
    inner = pl.BlockSpec(memory_space=pltpu.VMEM)
    per_chunk = pltpu.SemaphoreType.DMA((2, chunks))
    operands = (
        x_in,
        by_group(bc_in),
        gate_z,
        log_decay.transpose(0, 2, 1),
        resets[None, :],
        conv_x,
        by_group(conv_bc),
        skip_d[None, :],
        norm_gain[None, :],
        visit_span.T,
    )
    places = [pltpu.VMEM(v.shape, v.dtype) for v in operands]
    places[1] = pltpu.VMEM(((tokens + HALO) * pairs, STATE), bf16)
    made, pooled = pl.pallas_call(
        functools.partial(kernel, lax.axis_size("ctx"), groups),
        out_shape=(
            pltpu.VMEM((tokens, channels), bf16),
            pltpu.VMEM((vis, channels), bf16),
        ),
        in_specs=[outside] * 10,
        out_specs=(inner, inner),
        scratch_shapes=[
            *places,
            pltpu.VMEM((HALO, channels), bf16),
            pltpu.VMEM((HALO, channels), bf16),
            pltpu.VMEM((HALO * pairs, STATE), bf16),
            pltpu.VMEM((2, vis), jnp.int32),
            pltpu.VMEM((tokens * pairs, STATE), f32),
            pltpu.VMEM((groups, tokens, width), bf16),
            pltpu.VMEM((groups, tokens, STATE), bf16),
            pltpu.VMEM((groups, STATE, tokens), bf16),
            pltpu.VMEM((groups, tokens, STATE), bf16),
            pltpu.VMEM((groups, tokens, 2 * PER), f32),
            pltpu.VMEM((groups, 2 * PER, tokens), f32),
            pltpu.VMEM((groups, tokens, 8 * PER), bf16),
            pltpu.VMEM((groups, 2 * PER, 128), f32),
            pltpu.VMEM((2, 8 * PER, 2 * width), bf16),
            pltpu.VMEM((tokens, 2 * width), f32),
            pltpu.VMEM((tokens, 2 * width), bf16),
            pltpu.VMEM((4, tokens + HALO, 128), f32),
            pltpu.VMEM((groups, 8, width), f32),
            pltpu.VMEM((groups, tokens, width), f32),
            pltpu.VMEM((tokens, 128), f32),
            pltpu.VMEM(state, bf16),
            pltpu.VMEM((2, *with_end), bf16),
            pltpu.VMEM(with_end, bf16),
            pltpu.VMEM(state, bf16),
            pltpu.VMEM(state, bf16),
            pltpu.VMEM(state, bf16),
            pltpu.VMEM((groups, vis, width), f32),
            pltpu.VMEM((groups, vis, width), f32),
            pltpu.VMEM((groups, vis, width), f32),
            pltpu.SemaphoreType.DMA((11,)),
            pltpu.SemaphoreType.DMA((groups,)),
            pltpu.SemaphoreType.DMA((2, 2 + groups)),
            per_chunk, per_chunk, per_chunk,
            pltpu.SemaphoreType.DMA((2, groups)),
        ],
        compiler_params=pltpu.CompilerParams(
            collective_id=0, has_side_effects=True, vmem_limit_bytes=LIMIT << 20
        ),
    )(*operands)

    return pl.pallas_call(
        ship,
        out_shape=(
            jax.ShapeDtypeStruct((tokens, channels), bf16),
            jax.ShapeDtypeStruct((vis, channels), bf16),
        ),
        in_specs=[inner, inner],
        out_specs=[pl.BlockSpec(memory_space=pl.ANY)] * 2,
        scratch_shapes=[pltpu.SemaphoreType.DMA((2,))],
        compiler_params=pltpu.CompilerParams(vmem_limit_bytes=1 << 20),
    )(pltpu.with_memory_space_constraint(made, pltpu.VMEM), pltpu.with_memory_space_constraint(pooled, pltpu.VMEM))


def solution(mesh):
    return jax.shard_map(
        on_device,
        mesh=mesh,
        in_specs=(
            P(("groups", "ctx", "dp"), "tp"),
            P(("groups", "ctx", "dp"), None, "tp"),
            P(("groups", "ctx", "dp"), "tp"),
            P(None, ("groups", "ctx", "dp"), "tp"),
            P(("groups", "ctx", "dp")),
            P(None, "tp"),
            P(None, None, "tp"),
            P("tp"),
            P("tp"),
            P(("groups", "ctx", "dp"), None),
        ),
        out_specs=(P(("groups", "ctx", "dp"), "tp"), P(("groups", "ctx", "dp"), "tp")),
        check_vma=False,
    )
```

```python
import functools
import jax
import jax.numpy as jnp
from jax import lax
from jax.experimental import pallas as pl
from jax.experimental.pallas import tpu as pltpu
from jax.sharding import PartitionSpec as P

HEADDIM = 64
STATE = 128
GROUPS = 8
PER = 16
PARTS = 4
LOG2E = 1.4426950408889634
BIG = 160.0
LIMIT = 60
HALO = 8
LAG = 2
MESH = pl.DeviceIdType.MESH


def silu(v):
    half = 0.5 * v
    return half + half * jnp.tanh(half)


def conv(padded, taps):
    total = taps[3] * padded[HALO:]
    for k in range(3):
        total = total + taps[k] * pltpu.roll(padded, 3 - k, 0)[HALO:]
    return silu(total)


def dot(a, b):
    return jnp.dot(a, b, preferred_element_type=jnp.float32)


def kernel(
    chips,
    groups,
    x_hbm, bc_hbm, gate_hbm, rate_hbm, reset_hbm, taps_x_hbm, taps_bc_hbm, skip_hbm, gain_hbm, span_hbm,
    out_ref, pool_ref,
    x_ref, bc_ref, gate_ref, rate_ref, reset_ref, taps_x, taps_bc, skip_ref, gain_ref, span_ref,
    halo_x, tail_x, tail_bc, span_in, bc_wide, xc, bs, bt, cs, colt, rowt, weights, ends, expand, spreads, sent, shifted, skips, y_acc, squares, h_lead,
    s_made, s_in, chain_in, follow_in, chain_out,
    own_pool, spill_out, spill_in,
    sem_in, sem_x, sem_halo, sem_s, sem_chain, sem_follow, sem_spill,
):
    tokens = x_ref.shape[0]
    width = PER * HEADDIM
    half = tokens // 2
    part = width // PARTS
    chunks = PARTS * groups
    pairs = 2 * groups
    c = lax.axis_index("ctx")
    d = lax.axis_index("dp")
    other = 1 - d
    nxt = c + 2 * d - 1
    prv = c - 2 * d + 1
    pos = d * c + (1 - d) * (chips - 1 - c)
    has_next = pos < chips - 1
    has_prev = pos > 0
    index = c * 2 + d
    last_index = chips * 2 - 1
    partner = {"ctx": c, "dp": other}
    halo_to = {"ctx": d * nxt + (1 - d) * c, "dp": other}
    spill_to = {"ctx": d * c + (1 - d) * nxt, "dp": other}
    follow_chain = {"ctx": nxt, "dp": d}

    barrier = pltpu.get_barrier_semaphore()

    @pl.when(has_next)
    def _():
        pl.semaphore_signal(barrier, inc=1, device_id={"ctx": nxt, "dp": other}, device_id_type=MESH)
        pl.semaphore_signal(barrier, inc=1, device_id={"ctx": nxt, "dp": d}, device_id_type=MESH)

    @pl.when(has_prev)
    def _():
        pl.semaphore_signal(barrier, inc=1, device_id={"ctx": prv, "dp": d}, device_id_type=MESH)

    pl.semaphore_signal(barrier, inc=1, device_id=partner, device_id_type=MESH)

    bc_main = bc_ref.at[pl.ds(HALO * pairs, tokens * pairs)]
    tail_rows = bc_hbm.at[pl.ds((tokens - HALO) * pairs, HALO * pairs)]
    sources = (rate_hbm, reset_hbm, bc_hbm, taps_bc_hbm, taps_x_hbm, gate_hbm, skip_hbm, gain_hbm, span_hbm,
               tail_rows, x_hbm.at[pl.ds(tokens - HALO, HALO)])
    places = (rate_ref, reset_ref, bc_main, taps_bc, taps_x, gate_ref, skip_ref, gain_ref, span_ref,
              tail_bc, tail_x)
    loads = [pltpu.make_async_copy(sources[k], places[k], sem_in.at[k]) for k in range(11)]

    def x_load(g):
        wide = pl.ds(pl.multiple_of(g * width, width), width)
        return pltpu.make_async_copy(x_hbm.at[:, wide], x_ref.at[:, wide], sem_x.at[g])

    for load in loads[9:]:
        load.start()
    for load in (*loads[:5], loads[6]):
        load.start()
    x_load(0).start()

    rows = lax.broadcasted_iota(jnp.int32, (tokens, tokens), 0)
    cols = lax.broadcasted_iota(jnp.int32, (tokens, tokens), 1)
    upto = (rows <= cols).astype(jnp.float32).astype(jnp.bfloat16)
    erow = lax.broadcasted_iota(jnp.int32, (8 * PER, width), 0)
    ehead = lax.div(lax.broadcasted_iota(jnp.int32, (8 * PER, width), 1), HEADDIM)
    for which in range(4):
        least = 4 * PER * (which // 2)
        near = lax.rem(erow, 2 * PER) == ehead + PER * (1 - which % 2)
        near = near & (erow >= least) & (erow < least + 4 * PER)
        at = (which % 2) * width
        expand[which // 2, :, at : at + width] = near.astype(jnp.float32).astype(jnp.bfloat16)

    shifted[:, :HALO, :] = jnp.zeros((4, HALO, 128), jnp.float32)

    @pl.when(pos == 0)
    def _():
        chain_in[...] = jnp.zeros_like(chain_in)

    @pl.when(pos == chips - 1)
    def _():
        follow_in[...] = jnp.zeros_like(follow_in)

    @pl.when(index == 0)
    def _():
        halo_x[...] = jnp.zeros_like(halo_x)
        bc_ref[: HALO * pairs] = jnp.zeros((HALO * pairs, STATE), jnp.bfloat16)
        span_in[...] = jnp.zeros_like(span_in)

    for load in loads[:2]:
        load.wait()

    def hi_lo(v):
        hi = v.astype(jnp.bfloat16).astype(jnp.float32)
        return jnp.concatenate([hi, v - hi], axis=0)

    fold = BIG * reset_ref[...].astype(jnp.float32)
    heads = groups * PER
    rate = jnp.concatenate([rate_ref[0], rate_ref[1]], axis=0)
    step = rate * LOG2E - fold
    step_hi = step.astype(jnp.bfloat16)
    rest = step - step_hi.astype(jnp.float32)
    step_mid = rest.astype(jnp.bfloat16)
    step_lo = (rest - step_mid.astype(jnp.float32)).astype(jnp.bfloat16)
    sums = dot(jnp.concatenate([step_hi, step_mid, step_lo], axis=0), upto)
    cum = sums[: 2 * heads] + (sums[2 * heads : 4 * heads] + sums[4 * heads :])
    is_fwd = lax.broadcasted_iota(jnp.int32, (2 * heads, tokens), 0) < heads
    r = -2.0 * rate
    small = r * (1.0 - r * (1 / 2 - r * (1 / 6 - r * (1 / 24 - r * (1 / 120 - r / 720)))))
    loss = jnp.where(r < 0.25, small, 1.0 - jnp.exp(-r))
    log_weight = jnp.maximum((0.5 * LOG2E) * jnp.log(loss), -1000.0)
    col = jnp.where(is_fwd, cum, -cum)
    row = log_weight - col
    end = cum[:, tokens - 1 : tokens]
    to_end = jnp.exp2(row + jnp.where(is_fwd, end, 0.0))
    lead = jnp.exp2(jnp.where(is_fwd, cum, end - cum))
    total = jnp.broadcast_to(jnp.exp2(end), (2 * heads, 128))

    def of_group(v, g):
        return jnp.concatenate([v[g * PER : (g + 1) * PER], v[heads + g * PER : heads + (g + 1) * PER]], axis=0)

    for g in range(groups):
        colt[g] = of_group(col, g).T
        rowt[g] = of_group(row, g)
        ends[g] = of_group(total, g)
        both = jnp.concatenate([hi_lo(of_group(to_end, g)), hi_lo(of_group(lead, g))], axis=0)
        weights[g] = both.T.astype(jnp.bfloat16)

    pl.semaphore_wait(barrier, 1 + 2 * has_next.astype(jnp.int32) + has_prev.astype(jnp.int32))

    def remote(src, dst, sems, k, to):
        return pltpu.make_async_remote_copy(
            src_ref=src, dst_ref=dst, send_sem=sems.at[0, k], recv_sem=sems.at[1, k],
            device_id=to, device_id_type=MESH,
        )

    def halo_of(g):
        wide = pl.ds(pl.multiple_of(g * width, width), width)
        return remote(tail_x.at[:, wide], halo_x.at[:, wide], sem_halo, 2 + g, halo_to)

    halo_bc = remote(tail_bc, bc_ref.at[pl.ds(0, HALO * pairs)], sem_halo, 0, halo_to)
    halo_span = remote(span_hbm, span_in, sem_halo, 1, halo_to)

    for load in loads[9:]:
        load.wait()

    @pl.when(index < last_index)
    def _():
        halo_bc.start()
        for g in range(groups):
            halo_of(g).start()
        halo_span.start()

    for g in range(1, groups):
        x_load(g).start()

    def s_copy(q):
        return remote(s_made.at[0, q], s_in.at[q], sem_s, q, partner)

    def chain_copy(q):
        return remote(chain_out.at[q], chain_in.at[q], sem_chain, q, follow_chain)

    def follow_copy(q):
        return remote(chain_in.at[q], follow_in.at[q], sem_follow, q, partner)

    def spill_copy(g):
        return remote(spill_out.at[g], spill_in.at[g], sem_spill, g, spill_to)

    for load in loads[2:5]:
        load.wait()

    def lanes(k):
        return slice(k * part, (k + 1) * part)

    def lanes_of(which, k):
        return slice(which * width + k * part, which * width + (k + 1) * part)

    def spread_end(g, which, k):
        picked = expand[0, : 2 * PER, lanes_of(which, k)].astype(jnp.float32) * ends[g, :, :1]
        return jnp.broadcast_to(jnp.sum(picked, axis=0, keepdims=True), (8, part))

    def end_of(block):
        return block[STATE : STATE + 1].astype(jnp.float32) + block[STATE + 8 : STATE + 9].astype(jnp.float32)

    def relay(q):
        s_copy(q).wait_recv()

        @pl.when(has_prev)
        def _():
            chain_copy(q).wait_recv()
            follow_copy(q).start()

        near = s_in[q]
        state = end_of(near) * chain_in[q].astype(jnp.float32) + near[:STATE].astype(jnp.float32)
        h_lead[q] = state.astype(jnp.bfloat16)

        @pl.when(has_next)
        def _():
            own = s_made[1, q]
            chain_out[q] = (end_of(own) * state + own[:STATE].astype(jnp.float32)).astype(jnp.bfloat16)
            chain_copy(q).start()

    span = 32
    per_tap = [jnp.concatenate([taps_bc[k * pairs : (k + 1) * pairs]] * (span), axis=0) for k in range(4)]

    def conv_bc(t):
        at = pl.multiple_of(t * span * pairs, span * pairs)
        raw = bc_ref[pl.ds(at, (span + HALO) * pairs)].astype(jnp.float32)
        total = per_tap[3] * raw[HALO * pairs :]
        for k in range(3):
            back = (HALO - 3 + k) * pairs
            total = total + per_tap[k] * raw[back : back + span * pairs]
        bc_wide[pl.ds(at, span * pairs)] = silu(total)

    @pl.loop(1, tokens // span)
    def _(t):
        conv_bc(t)

    def conv_x(g, above, rows_at, k):
        wide = pl.ds(pl.multiple_of(g * width + k * part, part), part)
        padded = jnp.concatenate([above, x_ref[rows_at, wide].astype(jnp.float32)], axis=0)
        made = conv(padded, [taps_x[j : j + 1, wide] for j in range(4)])
        xc[g, rows_at, lanes(k)] = made.astype(jnp.bfloat16)

    def conv_below(g):
        x_load(g).wait()
        for k in range(width // 128):
            wide = pl.ds(pl.multiple_of(g * width + k * 128, 128), 128)
            slot = k % 4
            shifted[slot, HALO:, :] = x_ref[:, wide].astype(jnp.float32)
            total = taps_x[3:4, wide] * shifted[slot, HALO:, :]
            for j in range(3):
                total = total + taps_x[j : j + 1, wide] * shifted[slot, HALO - 3 + j : HALO - 3 + j + tokens, :]
            xc[g, :, k * 128 : (k + 1) * 128] = silu(total).astype(jnp.bfloat16)

    conv_below(0)
    loads[6].wait()

    @pl.loop(0, groups)
    def _(g):
        at = lax.broadcasted_iota(jnp.int32, (groups * PER, width), 0)
        head = lax.div(lax.broadcasted_iota(jnp.int32, (groups * PER, width), 1), HEADDIM)
        pick = (at == head + g * PER).astype(jnp.float32)
        skips[g] = lax.dot(jnp.broadcast_to(skip_ref[...], (8, groups * PER)), pick,
                           precision=lax.Precision.HIGHEST, preferred_element_type=jnp.float32)

    @pl.when(index > 0)
    def _():
        halo_bc.wait_recv()

    conv_bc(0)
    for load in (loads[5], *loads[7:9]):
        load.start()

    for g in range(groups):
        b_g = bc_wide[pl.ds(2 * g, tokens, stride=pairs), :]
        bs[g] = b_g.astype(jnp.bfloat16)
        bt[g] = b_g.T.astype(jnp.bfloat16)
        cs[g] = bc_wide[pl.ds(2 * g + 1, tokens, stride=pairs), :].astype(jnp.bfloat16)

    early = jnp.where(d == 0, 870 + 300 * (pos - 1), 850 + 300 * (pos - 1))

    def due_at(time):
        return jnp.clip(lax.div(time - early + 7800, 78) - 99, 0, chunks)

    def due_first(g):
        return jnp.where(pos == 0, jnp.clip(g * PARTS + PARTS - LAG, 0, chunks), due_at(1050 - 140 * (groups - 1 - g)))

    def due(unit):
        return jnp.where(pos == 0, chunks, due_at(1050 + 52 * unit))

    @pl.loop(0, groups)
    def _(g):
        spreads[...] = dot(weights[g], expand[0])

        @pl.when(index > 0)
        def _():
            halo_of(g).wait_recv()

        for k in range(PARTS):
            wide = pl.ds(pl.multiple_of(g * width + k * part, part), part)
            conv_x(g, halo_x[:, wide].astype(jnp.float32), slice(0, 16), k)
            xf = xc[g, :, lanes(k)].astype(jnp.float32)
            for which in range(2):
                sent[:, lanes_of(which, k)] = (xf * spreads[:, lanes_of(which, k)]).astype(jnp.bfloat16)
        made = dot(bt[g], sent[...]).astype(jnp.bfloat16)
        for k in range(PARTS):
            q = g * PARTS + k
            for which in range(2):
                role = d if which == 0 else other
                s_made[1 - role, q, :STATE] = made[:, lanes_of(which, k)]
                s_made[1 - role, q, STATE:] = hi_lo(spread_end(g, which, k)).astype(jnp.bfloat16)
            s_copy(q).start()

        @pl.loop(jnp.where(g == 0, 0, due_first(g - 1)), due_first(g))
        def _(q):
            relay(q)

        @pl.when(g < groups - 1)
        def _():
            conv_below(g + 1)

    @pl.when(pos == 0)
    def _():
        @pl.loop(max(chunks - LAG, 0), chunks)
        def _(q):
            relay(q)

    left = lax.broadcasted_iota(jnp.int32, (tokens, 128), 1) < HEADDIM
    lower = rows[:half, :half] >= cols[:half, :half]

    @pl.loop(0, groups)
    def _(g):
        score = lax.dot_general(cs[g], bs[g], (((1,), (1,)), ((), ())), preferred_element_type=jnp.float32)
        for quarter in range(2):
            unit = 4 * g + 2 * quarter + 1
            @pl.loop(jnp.where(unit == 1, jnp.where(pos == 0, chunks, due_first(groups - 1)), due(unit - 2)), due(unit))
            def _(q):
                relay(q)

            for pair in range(quarter * PER // 4, (quarter + 1) * PER // 4):
                at = pair * 2 * HEADDIM
                x_pair = xc[g, :, at : at + 2 * HEADDIM]
                got = []
                for head in (2 * pair, 2 * pair + 1):
                    cf = colt[g, :, head : head + 1]
                    cb = colt[g, :, PER + head : PER + head + 1]
                    rf = rowt[g, head : head + 1, :]
                    rb = rowt[g, PER + head : PER + head + 1, :]
                    tl = jnp.where(lower, cf[:half] + rf[:, :half], cb[:half] + rb[:, :half])
                    tr = cb[:half] + rb[:, half:]
                    bl = cf[half:] + rf[:, :half]
                    br = jnp.where(lower, cf[half:] + rf[:, half:], cb[half:] + rb[:, half:])
                    top = jnp.concatenate([tl, tr], axis=1)
                    bottom = jnp.concatenate([bl, br], axis=1)
                    mix_top = (score[:half] * jnp.exp2(top)).astype(jnp.bfloat16)
                    mix_bottom = (score[half:] * jnp.exp2(bottom)).astype(jnp.bfloat16)
                    got.append(dot(jnp.concatenate([mix_top, mix_bottom], axis=0), x_pair))
                y_acc[g, :, at : at + 2 * HEADDIM] = jnp.where(left, got[0], got[1])

    for load in (loads[5], *loads[7:9]):
        load.wait()

    @pl.when(index > 0)
    def _():
        halo_span.wait_recv()

    vis = span_ref.shape[1]
    token = index * tokens + lax.broadcasted_iota(jnp.int32, (tokens, vis), 0)

    def covers(ref):
        return ((token >= ref[0:1]) & (token < ref[1:2])).astype(jnp.float32).T

    inside = jnp.concatenate([covers(span_ref), covers(span_in)], axis=0).astype(jnp.bfloat16)
    same = lax.broadcasted_iota(jnp.int32, (vis, vis), 0) == lax.broadcasted_iota(jnp.int32, (vis, vis), 1)
    spanned = jnp.maximum(span_ref[1:2] - span_ref[0:1], 1).astype(jnp.float32)
    length = jnp.sum(jnp.where(same, spanned, 0.0), axis=1, keepdims=True)

    before = due(4 * groups - 1)

    def reached(step):
        further = before + lax.div(step, 1) + 1
        return jnp.clip(jnp.maximum(step + 1, jnp.where(has_next, further, before)), 0, chunks)

    def all_sent(g):
        for k in range(PARTS):
            q = g * PARTS + k
            s_copy(q).wait_send()

            @pl.when(has_prev)
            def _():
                follow_copy(q).wait_send()

            @pl.when(has_next)
            def _():
                chain_copy(q).wait_send()

    @pl.loop(0, groups)
    def _(g):
        @pl.when(g > 0)
        def _():
            all_sent(g - 1)

        spreads[...] = dot(weights[g], expand[1])
        for k in range(PARTS // 2):
            q = g * PARTS + 2 * k

            @pl.loop(jnp.where(q == 0, before, reached(q - 1)), reached(q + 1))
            def _(p):
                relay(p)

            @pl.when(has_next)
            def _():
                follow_copy(q).wait_recv()
                follow_copy(q + 1).wait_recv()

            wide = pl.ds(pl.multiple_of(g * width + 2 * k * part, part), 2 * part)
            near = pl.ds(pl.multiple_of(d * width + 2 * k * part, part), 2 * part)
            far = pl.ds(pl.multiple_of(other * width + 2 * k * part, part), 2 * part)
            here = slice(2 * k * part, (2 * k + 2) * part)
            c_g = cs[g]
            lead = spreads[:, near] * dot(c_g, jnp.concatenate([h_lead[q], h_lead[q + 1]], axis=1))
            lead = lead + spreads[:, far] * dot(c_g, jnp.concatenate([follow_in[q], follow_in[q + 1]], axis=1))
            mixed = y_acc[g, :, here] + lead + skips[g, 0:1, here] * xc[g, :, here].astype(jnp.float32)
            gated = mixed * silu(gate_ref[:, wide].astype(jnp.float32))
            y_acc[g, :, here] = gated
            square = gated * gated
            folded = square[:, :128]
            for n in range(1, part // 64):
                folded = folded + square[:, n * 128 : (n + 1) * 128]
            if k == 0:
                squares[...] = folded
            else:
                squares[...] += folded

        mean_sq = jnp.sum(squares[...], axis=1, keepdims=True) * (1.0 / width)
        scale = lax.rsqrt(mean_sq + 1e-05)
        for k in range(PARTS):
            wide = pl.ds(pl.multiple_of(g * width + k * part, part), part)
            token_out = (y_acc[g, :, lanes(k)] * scale * gain_ref[:, wide]).astype(jnp.bfloat16)
            out_ref[:, wide] = token_out
            sums = dot(inside, token_out)
            own_pool[g, :, lanes(k)] = sums[:vis]
            spill_out[g, :, lanes(k)] = sums[vis:]

        @pl.when(index > 0)
        def _():
            spill_copy(g).start()

    @pl.loop(0, groups)
    def _(g):
        wide = pl.ds(pl.multiple_of(g * width, width), width)

        @pl.when(index < last_index)
        def _():
            spill_copy(g).wait_recv()
            pool_ref[:, wide] = ((own_pool[g] + spill_in[g]) / length).astype(jnp.bfloat16)

        @pl.when(index == last_index)
        def _():
            pool_ref[:, wide] = (own_pool[g] / length).astype(jnp.bfloat16)

    all_sent(groups - 1)

    @pl.when(index > 0)
    def _():
        @pl.loop(0, groups)
        def _(g):
            spill_copy(g).wait_send()

    @pl.when(index < last_index)
    def _():
        halo_bc.wait_send()
        halo_span.wait_send()
        for g in range(groups):
            halo_of(g).wait_send()


def ship(made_ref, pool_ref, out_ref, out_pool_ref, sems):
    copies = (
        pltpu.make_async_copy(made_ref, out_ref, sems.at[0]),
        pltpu.make_async_copy(pool_ref, out_pool_ref, sems.at[1]),
    )
    for copy in copies:
        copy.start()
    for copy in copies:
        copy.wait()


def on_device(
    x_in, bc_in, gate_z, log_decay, resets, conv_x, conv_bc, skip_d, norm_gain, visit_span
):
    tokens, channels = x_in.shape
    groups = bc_in.shape[2] // STATE
    width = PER * HEADDIM
    part = width // PARTS
    vis = visit_span.shape[0]
    chunks = PARTS * groups
    pairs = 2 * groups

    def by_group(v):
        return v.reshape(v.shape[0], 2, groups, STATE).transpose(0, 2, 1, 3).reshape(-1, STATE)

    f32, bf16 = jnp.float32, jnp.bfloat16
    state = (chunks, STATE, part)
    with_end = (chunks, STATE + 16, part)
    outside = pl.BlockSpec(memory_space=pltpu.HBM)
    inner = pl.BlockSpec(memory_space=pltpu.VMEM)
    per_chunk = pltpu.SemaphoreType.DMA((2, chunks))
    operands = (
        x_in,
        by_group(bc_in),
        gate_z,
        log_decay.transpose(0, 2, 1),
        resets[None, :],
        conv_x,
        by_group(conv_bc),
        skip_d[None, :],
        norm_gain[None, :],
        visit_span.T,
    )
    places = [pltpu.VMEM(v.shape, v.dtype) for v in operands]
    places[1] = pltpu.VMEM(((tokens + HALO) * pairs, STATE), bf16)
    made, pooled = pl.pallas_call(
        functools.partial(kernel, lax.axis_size("ctx"), groups),
        out_shape=(
            pltpu.VMEM((tokens, channels), bf16),
            pltpu.VMEM((vis, channels), bf16),
        ),
        in_specs=[outside] * 10,
        out_specs=(inner, inner),
        scratch_shapes=[
            *places,
            pltpu.VMEM((HALO, channels), bf16),
            pltpu.VMEM((HALO, channels), bf16),
            pltpu.VMEM((HALO * pairs, STATE), bf16),
            pltpu.VMEM((2, vis), jnp.int32),
            pltpu.VMEM((tokens * pairs, STATE), f32),
            pltpu.VMEM((groups, tokens, width), bf16),
            pltpu.VMEM((groups, tokens, STATE), bf16),
            pltpu.VMEM((groups, STATE, tokens), bf16),
            pltpu.VMEM((groups, tokens, STATE), bf16),
            pltpu.VMEM((groups, tokens, 2 * PER), f32),
            pltpu.VMEM((groups, 2 * PER, tokens), f32),
            pltpu.VMEM((groups, tokens, 8 * PER), bf16),
            pltpu.VMEM((groups, 2 * PER, 128), f32),
            pltpu.VMEM((2, 8 * PER, 2 * width), bf16),
            pltpu.VMEM((tokens, 2 * width), f32),
            pltpu.VMEM((tokens, 2 * width), bf16),
            pltpu.VMEM((4, tokens + HALO, 128), f32),
            pltpu.VMEM((groups, 8, width), f32),
            pltpu.VMEM((groups, tokens, width), f32),
            pltpu.VMEM((tokens, 128), f32),
            pltpu.VMEM(state, bf16),
            pltpu.VMEM((2, *with_end), bf16),
            pltpu.VMEM(with_end, bf16),
            pltpu.VMEM(state, bf16),
            pltpu.VMEM(state, bf16),
            pltpu.VMEM(state, bf16),
            pltpu.VMEM((groups, vis, width), f32),
            pltpu.VMEM((groups, vis, width), f32),
            pltpu.VMEM((groups, vis, width), f32),
            pltpu.SemaphoreType.DMA((11,)),
            pltpu.SemaphoreType.DMA((groups,)),
            pltpu.SemaphoreType.DMA((2, 2 + groups)),
            per_chunk, per_chunk, per_chunk,
            pltpu.SemaphoreType.DMA((2, groups)),
        ],
        compiler_params=pltpu.CompilerParams(
            collective_id=0, has_side_effects=True, vmem_limit_bytes=LIMIT << 20
        ),
    )(*operands)

    return pl.pallas_call(
        ship,
        out_shape=(
            jax.ShapeDtypeStruct((tokens, channels), bf16),
            jax.ShapeDtypeStruct((vis, channels), bf16),
        ),
        in_specs=[inner, inner],
        out_specs=[pl.BlockSpec(memory_space=pl.ANY)] * 2,
        scratch_shapes=[pltpu.SemaphoreType.DMA((2,))],
        compiler_params=pltpu.CompilerParams(vmem_limit_bytes=1 << 20),
    )(pltpu.with_memory_space_constraint(made, pltpu.VMEM), pltpu.with_memory_space_constraint(pooled, pltpu.VMEM))


def solution(mesh):
    return jax.shard_map(
        on_device,
        mesh=mesh,
        in_specs=(
            P(("groups", "ctx", "dp"), "tp"),
            P(("groups", "ctx", "dp"), None, "tp"),
            P(("groups", "ctx", "dp"), "tp"),
            P(None, ("groups", "ctx", "dp"), "tp"),
            P(("groups", "ctx", "dp")),
            P(None, "tp"),
            P(None, None, "tp"),
            P("tp"),
            P("tp"),
            P(("groups", "ctx", "dp"), None),
        ),
        out_specs=(P(("groups", "ctx", "dp"), "tp"), P(("groups", "ctx", "dp"), "tp")),
        check_vma=False,
    )
```
